32 devices in a mesh: snap: 4 (over z), vert: 8 (over y, x, core).
Axes of the slice: x: 2, y: 2, z: 4, core: 2. Of those that a mesh axis runs over, the one named last changes fastest.
Arguments:
- features: bfloat16 [4, 6144, 128], P('snap', 'vert'), may hold values from -6 to 6
- adjacency_tiles: bfloat16 [4, 96, 128, 128], P('snap', 'vert'), may hold values from -0.375 to 0.375
- src_block: int32 [4, 96], P('snap', 'vert'), may hold values from 0 to 47, as said below
- dst_block: int32 [4, 96], P('snap', 'vert'), may hold values from 0 to 5
- block_count: int32 [4, 8], P('snap', 'vert'), may hold values from 6 to 12, as said below
- w_conv: bfloat16 [128, 512], replicated, may hold values from -0.5 to 0.5
- b_conv: float32 [512], replicated, may hold values from -3 to 3
- w_input: bfloat16 [512, 2048], replicated, may hold values from -0.25 to 0.25
- w_state: bfloat16 [512, 2048], replicated, may hold values from -0.25 to 0.25
- b_gates: float32 [2048], replicated, may hold values from -3 to 3
Outputs:
- hidden_seq: bfloat16 [4, 6144, 512], P('snap', 'vert')
The draws below stay inside these ranges and needn't reach their ends.
Inputs may be any that keep to these rules, and one draw needn't show every extreme that they name: `src_block`: slot s of owner v names a column block held by owner v - 1, v or v + 1 (clipped to the owners that exist); its first slot names one of owner v - 1 and its second one of owner v + 1 where those exist. `block_count`: in every snapshot some owner has all 12 slots live.
All inputs are finite; a program needn't handle non-finite values.
Results may differ from the reference program's by a relative error of at most 0.0044.
Values may be sent and summed in bfloat16 or wider, within the bound.
No kernel may reach another device: no remote copies, remote signals or barrier semaphores. Data moves between devices by JAX's collectives and lax.ppermute only.
A program may use at most 64 MiB of HBM per device.

```python
import jax
import jax.numpy as jnp
from jax import lax

F = 128
P_SIZE = 512
HID = 512
BLOCK = 128
V_DEV = 768
SNAPS = 4
VERTS = 6144
RBLK = 6
EBLK = 12
N_VERT = 8


def draw_src_block(key, part):
    owners = VERTS // V_DEV
    shape = (SNAPS, owners, EBLK)
    owner_grid = jnp.broadcast_to(jnp.arange(owners, dtype=jnp.int32)[None, :, None], shape)
    offsets = jax.random.randint(jax.random.fold_in(key, 11), shape, -1, 2)
    slot_grid = jnp.broadcast_to(jnp.arange(EBLK, dtype=jnp.int32)[None, None, :], shape)
    offsets = jnp.where(slot_grid == 0, -1, jnp.where(slot_grid == 1, 1, offsets))
    target = jnp.clip(owner_grid + offsets, 0, owners - 1)
    within = jax.random.randint(jax.random.fold_in(key, 12), shape, 0, RBLK)
    return (target * RBLK + within).reshape(SNAPS, owners * EBLK).astype(jnp.int32)


def draw_block_count(key, part):
    owners = VERTS // V_DEV
    lowest = max(2, EBLK // 2)
    counts = jax.random.randint(jax.random.fold_in(key, 21), (SNAPS, owners), lowest, EBLK + 1)
    fullest = jax.random.randint(jax.random.fold_in(key, 22), (SNAPS, 1), 0, owners)
    columns = jnp.arange(owners, dtype=jnp.int32)[None, :]
    return jnp.where(columns == fullest, EBLK, counts).astype(jnp.int32)


def set_ends(drawn, stream_key, least, top_value):
    dims = drawn.shape
    place = [jax.random.randint(jax.random.fold_in(stream_key, axis), (), 0, dims[axis]) for axis in range(len(dims))]
    drawn = drawn.at[tuple(place)].set(least)
    longest = dims.index(max(dims))
    place[longest] = (place[longest] + 1) % dims[longest]
    return drawn.at[tuple(place)].set(top_value)


def steps_of(stream_key, shape, split, low, top_value):
    loudness, own = 1.0, jax.random.fold_in(stream_key, 6)
    for dim, shards_of in split:
        draws = jnp.exp(jax.random.uniform(jax.random.fold_in(own, dim), (shards_of,), jnp.float32, low / len(split), top_value / len(split)))
        loudness = loudness * jnp.repeat(draws, shape[dim] // shards_of).reshape([-1 if axis == dim else 1 for axis in range(len(shape))])
    return loudness


def centred(own_key, extent, spread, most, cuts=(), kind=jnp.bfloat16):
    drawn = jax.random.normal(own_key, extent, jnp.float32) * spread
    if len(cuts) > 0:
        drawn = steps_of(own_key, extent, cuts, -0.22, 0.18) * drawn
    return jnp.clip(drawn, min=-most, max=most).astype(kind)


def setup_inputs(seed: int = 0) -> dict:
    seeds = jax.random.split(jax.random.key(seed), 11)
    features = centred(seeds[0], (SNAPS, VERTS, F), 1.0, 6.0, ((0, 4), (1, 8)))
    adjacency_tiles = centred(seeds[1], (SNAPS, N_VERT * EBLK, BLOCK, BLOCK), (2 * BLOCK) ** -0.5, 0.375, ((0, 4), (1, 8)))
    src_block = draw_src_block(jax.random.fold_in(seeds[10], 71), 0)
    dst_block = set_ends(jax.random.randint(seeds[3], (SNAPS, N_VERT * EBLK), 0, RBLK), jax.random.fold_in(seeds[3], 1), 0, RBLK - 1).astype(jnp.int32)
    block_count = draw_block_count(jax.random.fold_in(seeds[10], 71), 0)
    w_conv = centred(seeds[5], (F, P_SIZE), F ** -0.5, 0.5)
    b_conv = centred(seeds[6], (P_SIZE,), 0.5, 3.0, (), jnp.float32)
    w_input = centred(seeds[7], (P_SIZE, 4 * HID), P_SIZE ** -0.5, 0.25)
    w_state = centred(seeds[8], (HID, 4 * HID), HID ** -0.5, 0.25)
    b_gates = centred(seeds[9], (4 * HID,), 0.5, 3.0, (), jnp.float32)
    return {"features": features, "adjacency_tiles": adjacency_tiles, "src_block": src_block, "dst_block": dst_block, "block_count": block_count, "w_conv": w_conv, "b_conv": b_conv, "w_input": w_input, "w_state": w_state, "b_gates": b_gates}


forget_bias = 2.0


def reference(features, adjacency_tiles, src_block, dst_block, block_count, w_conv, b_conv, w_input, w_state, b_gates):
    owners = VERTS // V_DEV
    nblocks = VERTS // BLOCK
    slots = jnp.arange(owners * EBLK, dtype=jnp.int32)
    owner_of = slots // EBLK
    position = slots % EBLK

    def advance(carry, inputs):
        hidden, cell = carry
        feats, tiles_now, sources, targets, counts = inputs
        blocks = feats.reshape(nblocks, BLOCK, F)
        picked = blocks[sources]
        product = jnp.einsum('ebk,ekf->ebf', tiles_now.astype(jnp.float32), picked.astype(jnp.float32), precision=lax.Precision.HIGHEST)
        alive = (position < counts[owner_of]).astype(jnp.float32)
        row_target = (owner_of * RBLK + targets).astype(jnp.int32)
        summed = jax.ops.segment_sum(product * alive[:, None, None], row_target, num_segments=nblocks)
        summed = summed.reshape(VERTS, F).astype(jnp.bfloat16)
        conv = jax.nn.relu(jnp.dot(summed, w_conv, preferred_element_type=jnp.float32) + b_conv).astype(jnp.bfloat16)
        gates = jnp.dot(conv, w_input, preferred_element_type=jnp.float32) + jnp.dot(hidden, w_state, preferred_element_type=jnp.float32) + b_gates
        input_gate = jax.nn.sigmoid(gates[:, :HID])
        forget_gate = jax.nn.sigmoid(gates[:, HID:2 * HID] + forget_bias)
        candidate = jnp.tanh(gates[:, 2 * HID:3 * HID])
        output_gate = jax.nn.sigmoid(gates[:, 3 * HID:])
        new_cell = forget_gate * cell + input_gate * candidate
        new_hidden = (output_gate * jnp.tanh(new_cell)).astype(jnp.bfloat16)
        return (new_hidden, new_cell), new_hidden

    start = (jnp.zeros((VERTS, HID), jnp.bfloat16), jnp.zeros((VERTS, HID), jnp.float32))
    _, sequence = lax.scan(advance, start, (features, adjacency_tiles, src_block, dst_block, block_count))
    return sequence
```

```python
import functools

import jax
import jax.numpy as jnp
from jax import lax
from jax.experimental import pallas as pl
from jax.experimental.pallas import tpu as pltpu
from jax.sharding import PartitionSpec as P

forget_bias = 2.0
BF16 = jnp.bfloat16
F32 = jnp.float32
VMEM = pl.BlockSpec(memory_space=pltpu.VMEM)
SMEM = pl.BlockSpec(memory_space=pltpu.SMEM)
ANY = pl.BlockSpec(memory_space=pl.ANY)


def aggregate_kernel(own, left, right, tiles, src, dst, count, whole, straight, cross, window, total):
    rows = own.shape[0]
    block = tiles.shape[1]
    slots = tiles.shape[0]
    row_blocks = rows // block
    half = rows // 2
    base = (lax.axis_index("vert") - 1) * row_blocks
    parity = lax.axis_index("snap") % 2
    window[0:rows] = left[...]
    window[rows : 2 * rows] = own[...]
    window[2 * rows : 3 * rows] = right[...]
    total[...] = jnp.zeros_like(total)
    products = []
    for slot in range(slots):
        column = jnp.clip(src[0, slot] - base, 0, 3 * row_blocks - 1)
        start = pl.multiple_of(column * block, block)
        products.append(
            jnp.dot(tiles[slot], window[pl.ds(start, block)], preferred_element_type=F32)
        )
    for slot in range(slots):
        start = pl.multiple_of(jnp.clip(dst[0, slot], 0, row_blocks - 1) * block, block)
        alive = slot < count[0, 0]
        total[pl.ds(start, block)] += jnp.where(alive, products[slot], 0.0)
    whole[...] = total[...].astype(BF16)
    near = pl.multiple_of(parity * half, half)
    far = pl.multiple_of((1 - parity) * half, half)
    straight[...] = total[pl.ds(near, half)].astype(BF16)
    cross[...] = total[pl.ds(far, half)].astype(BF16)


def aggregate(own, left, right, tiles, src, dst, count):
    rows, width = own.shape
    shape = jax.ShapeDtypeStruct
    return pl.pallas_call(
        aggregate_kernel,
        out_shape=(
            shape((rows, width), BF16),
            shape((rows // 2, width), BF16),
            shape((rows // 2, width), BF16),
        ),
        in_specs=[VMEM, VMEM, VMEM, VMEM, SMEM, SMEM, SMEM],
        out_specs=(VMEM, VMEM, VMEM),
        scratch_shapes=[pltpu.VMEM((3 * rows, width), BF16), pltpu.VMEM((rows, width), F32)],
        compiler_params=pltpu.CompilerParams(vmem_limit_bytes=8 << 20),
        name="aggregate",
    )(own, left, right, tiles, src, dst, count)


def recur_kernel(snaps, first, chunk, *refs):
    passed = 2 * (snaps // 2 - 1)
    own, pair = refs[:2]
    taken = refs[2 : 2 + passed]
    w_conv, b_conv, w_input, w_state, b_gates = refs[2 + passed : 7 + passed]
    out, rows_in, conv, hidden, cell, sem = refs[-6:]
    rows = rows_in.shape[0]
    width = w_state.shape[0]
    me = lax.axis_index("snap")
    parity = me % 2
    mine = parity if first else 1 - parity
    offset = pl.multiple_of(mine * rows, rows)
    for step in range(snaps):

        @pl.when(step <= me)
        def _(step=step):
            @pl.when(step == me)
            def _():
                rows_in[...] = own[pl.ds(offset, rows)]

            @pl.when((step == me - 1) & (parity == 1))
            def _():
                rows_in[...] = pair[pl.ds(offset, rows)]

            for ahead in range(1, snaps // 2 - step // 2):
                for turned in range(2):

                    @pl.when((me // 2 == step // 2 + ahead) & ((mine != step % 2) == (turned == 1)))
                    def _(ahead=ahead, turned=turned):
                        rows_in[...] = taken[2 * (ahead - 1) + turned][...]

            reached = jnp.dot(rows_in[...], w_conv[...], preferred_element_type=F32) + b_conv[...]
            conv[...] = jnp.maximum(reached, 0.0).astype(BF16)
            for low in range(0, width, chunk):
                gates = []
                for gate in range(4):
                    part = slice(gate * width + low, gate * width + low + chunk)
                    value = jnp.dot(conv[...], w_input[:, part], preferred_element_type=F32)
                    if step:
                        value += jnp.dot(
                            hidden[step % 2], w_state[:, part], preferred_element_type=F32
                        )
                    gates.append(value + b_gates[:, part])
                part = slice(low, low + chunk)
                fresh = (0.5 * jnp.tanh(0.5 * gates[0]) + 0.5) * jnp.tanh(gates[2])
                if step:
                    keep = 0.5 * jnp.tanh(0.5 * (gates[1] + forget_bias)) + 0.5
                    fresh += keep * cell[:, part]
                cell[:, part] = fresh
                shown = (0.5 * jnp.tanh(0.5 * gates[3]) + 0.5) * jnp.tanh(fresh)
                hidden[(step + 1) % 2, :, part] = shown.astype(BF16)

    copy = pltpu.make_async_copy(
        hidden.at[(me + 1) % 2], out.at[0, pl.ds(offset, rows)], sem
    )
    copy.start()
    copy.wait()


def recur(first, own, pair, taken, weights, before):
    rows = own.shape[0] // 2
    width = weights[3].shape[0]
    snaps = lax.axis_size("snap")
    operands = [own, pair, *taken, *weights]
    specs = [VMEM] * len(operands)
    aliases = {}
    if before is not None:
        aliases = {len(operands): 0}
        operands.append(before)
        specs.append(ANY)
    return pl.pallas_call(
        functools.partial(recur_kernel, snaps, first, width // 2),
        out_shape=jax.ShapeDtypeStruct((1, 2 * rows, width), BF16),
        in_specs=specs,
        out_specs=ANY,
        scratch_shapes=[
            pltpu.VMEM((rows, own.shape[1]), BF16),
            pltpu.VMEM((rows, weights[2].shape[0]), BF16),
            pltpu.VMEM((2, rows, width), BF16),
            pltpu.VMEM((rows, width), F32),
            pltpu.SemaphoreType.DMA,
        ],
        input_output_aliases=aliases,
        compiler_params=pltpu.CompilerParams(vmem_limit_bytes=40 << 20),
        cost_estimate=pl.CostEstimate(
            flops=14 * rows * width * width * snaps,
            transcendentals=5 * rows * width * snaps,
            bytes_accessed=8 * width * width * 2,
        ),
        name="recur_first" if first else "recur_second",
    )(*operands)


def shards(
    features,
    adjacency_tiles,
    src_block,
    dst_block,
    block_count,
    w_conv,
    b_conv,
    w_input,
    w_state,
    b_gates,
):
    own = features[0]
    owners = lax.axis_size("vert")
    snaps = lax.axis_size("snap")
    left = lax.ppermute(own, "vert", [(i, i + 1) for i in range(owners - 1)])
    right = lax.ppermute(own, "vert", [(i + 1, i) for i in range(owners - 1)])
    whole, straight, cross = aggregate(
        own, left, right, adjacency_tiles[0], src_block, dst_block, block_count
    )
    taken = []
    for ahead in range(1, snaps // 2):
        starts = [(i, b) for i in range(snaps // 2 - ahead) for b in range(2)]
        taken.append(
            lax.ppermute(straight, "snap", [(2 * i + b, 2 * (i + ahead) + b) for i, b in starts])
        )
        taken.append(
            lax.ppermute(cross, "snap", [(2 * i + b, 2 * (i + ahead) + 1 - b) for i, b in starts])
        )
    pair = lax.ppermute(whole, "snap", [(2 * i, 2 * i + 1) for i in range(snaps // 2)])
    swap = [(i, i ^ 1) for i in range(snaps)]
    swapped = [lax.ppermute(part, "snap", swap) for part in taken]
    weights = (w_conv, b_conv[None], w_input, w_state, b_gates[None])
    out = recur(True, whole, pair, taken, weights, None)
    return recur(False, whole, pair, swapped, weights, out)


def solution(mesh):
    placed = (
        P("snap", "vert", None),
        P("snap", "vert", None, None),
        P("snap", "vert"),
        P("snap", "vert"),
        P("snap", "vert"),
        P(),
        P(),
        P(),
        P(),
        P(),
    )
    return jax.shard_map(
        shards, mesh=mesh, in_specs=placed, out_specs=P("snap", "vert", None), check_vma=False
    )
```

```python
import functools

import jax
import jax.numpy as jnp
from jax import lax
from jax.experimental import pallas as pl
from jax.experimental.pallas import tpu as pltpu
from jax.sharding import PartitionSpec as P

forget_bias = 2.0
BF16 = jnp.bfloat16
F32 = jnp.float32
VMEM = pl.BlockSpec(memory_space=pltpu.VMEM)
SMEM = pl.BlockSpec(memory_space=pltpu.SMEM)
HBM = pl.BlockSpec(memory_space=pltpu.HBM)
GRANT = 24 << 20


def load_kernel(total, *refs):
    sems = refs[-1]
    copies = []
    for place in range(total):
        copies.append(
            pltpu.make_async_copy(refs[place], refs[total + place], sems.at[place])
        )
    for copy in copies:
        copy.start()
    for copy in copies:
        copy.wait()


def load(arrays):
    bytes_moved = sum(array.size * array.dtype.itemsize for array in arrays)
    return pl.pallas_call(
        functools.partial(load_kernel, len(arrays)),
        out_shape=[jax.ShapeDtypeStruct(array.shape, array.dtype) for array in arrays],
        in_specs=[HBM] * len(arrays),
        out_specs=[VMEM] * len(arrays),
        scratch_shapes=[pltpu.SemaphoreType.DMA((len(arrays),))],
        compiler_params=pltpu.CompilerParams(vmem_limit_bytes=GRANT),
        cost_estimate=pl.CostEstimate(
            flops=0, transcendentals=0, bytes_accessed=2 * bytes_moved
        ),
        name="load",
    )(*(pltpu.with_memory_space_constraint(array, pltpu.HBM) for array in arrays))


def aggregate_kernel(
    own, left, right, tiles, src_in, dst_in, count, whole, window, total, src, dst, sems
):
    lists = ((src_in, src), (dst_in, dst))
    copies = [pltpu.make_async_copy(a, b, sems.at[i]) for i, (a, b) in enumerate(lists)]
    for copy in copies:
        copy.start()
    rows = own.shape[0]
    block = tiles.shape[1]
    slots = tiles.shape[0]
    row_blocks = rows // block
    base = (lax.axis_index("vert") - 1) * row_blocks
    window[0:rows] = left[...]
    window[rows : 2 * rows] = own[...]
    window[2 * rows : 3 * rows] = right[...]
    total[...] = jnp.zeros_like(total)
    for copy in copies:
        copy.wait()
    products = []
    for slot in range(slots):
        column = jnp.clip(src[0, slot] - base, 0, 3 * row_blocks - 1)
        start = pl.multiple_of(column * block, block)
        products.append(
            jnp.dot(tiles[slot], window[pl.ds(start, block)], preferred_element_type=F32)
        )
    for slot in range(slots):
        start = pl.multiple_of(jnp.clip(dst[0, slot], 0, row_blocks - 1) * block, block)
        alive = slot < count[0, 0]
        total[pl.ds(start, block)] += jnp.where(alive, products[slot], 0.0)
    whole[...] = total[...].astype(BF16)


def aggregate(own, left, right, tiles, src, dst, count):
    rows, width = own.shape
    return pl.pallas_call(
        aggregate_kernel,
        out_shape=jax.ShapeDtypeStruct((rows, width), BF16),
        in_specs=[VMEM] * 4 + [HBM] * 2 + [SMEM],
        out_specs=VMEM,
        scratch_shapes=[
            pltpu.VMEM((3 * rows, width), BF16),
            pltpu.VMEM((rows, width), F32),
            *(pltpu.SMEM(array.shape, jnp.int32) for array in (src, dst)),
            pltpu.SemaphoreType.DMA((2,)),
        ],
        compiler_params=pltpu.CompilerParams(vmem_limit_bytes=GRANT),
        name="aggregate",
    )(own, left, right, tiles, src, dst, count)


def convolve(rows_in, w_conv, b_conv, conv):
    reached = jnp.dot(rows_in[...], w_conv[...], preferred_element_type=F32) + b_conv[...]
    conv[...] = jnp.maximum(reached, 0.0).astype(BF16)


def pregate_kernel(rows_in, w_conv, b_conv, w_input, pre, conv):
    convolve(rows_in, w_conv, b_conv, conv)
    width = w_input.shape[1] // 4
    for gate in range(4):
        part = slice(gate * width, (gate + 1) * width)
        pre[:, part] = jnp.dot(conv[...], w_input[:, part], preferred_element_type=F32)


def pregate(rows_in, w_conv, b_conv, w_input):
    rows = rows_in.shape[0]
    depth, gates = w_input.shape
    return pl.pallas_call(
        pregate_kernel,
        out_shape=jax.ShapeDtypeStruct((rows, gates), F32),
        in_specs=[VMEM] * 4,
        out_specs=VMEM,
        scratch_shapes=[pltpu.VMEM((rows, depth), BF16)],
        compiler_params=pltpu.CompilerParams(vmem_limit_bytes=GRANT),
        cost_estimate=pl.CostEstimate(
            flops=2 * rows * depth * gates, transcendentals=0, bytes_accessed=rows * gates * 4
        ),
        name="pregate",
    )(rows_in, w_conv, b_conv, w_input)


def gate_step(conv, pre, w_input, w_state, b_gates, hidden, cell, fresh_hidden, done, first):
    width = w_state.shape[0]
    chunk = width // 2
    for low in range(0, width, chunk):
        gates = []
        for gate in range(4):
            part = slice(gate * width + low, gate * width + low + chunk)
            if pre is None:
                value = jnp.dot(conv[...], w_input[:, part], preferred_element_type=F32)
            else:
                value = pre[:, part]
            if not first:
                value += jnp.dot(hidden[...], w_state[:, part], preferred_element_type=F32)
            bias = b_gates[:, part]
            if gate == 1:
                bias = bias + forget_bias
            gates.append(value + bias)
        part = slice(low, low + chunk)
        fresh = (0.5 * jnp.tanh(0.5 * gates[0]) + 0.5) * jnp.tanh(gates[2])
        if not first:
            fresh += (0.5 * jnp.tanh(0.5 * gates[1]) + 0.5) * cell[:, part]
        cell[:, part] = fresh
        shown = (0.5 * jnp.tanh(0.5 * gates[3]) + 0.5) * jnp.tanh(fresh)
        fresh_hidden[:, part] = shown.astype(BF16)
        if done is not None:
            done(part)


def step_kernel(on_first, on_later, on_own, carried, *refs):
    own_refs = 2 if on_own is not None else 1
    rows_in, w_conv, b_conv, w_input, w_state, b_gates = refs[:6]
    conv, spare = refs[-3:-1] if on_own is not None else refs[-2:]
    me = lax.axis_index("snap")
    start = 6 + (1 if on_own is not None else 0) + (2 if carried else 0)
    if on_own is not None:
        pre = refs[6]
        out = refs[start]
        hidden, cell = refs[start + 1 : start + 3]
        sems = refs[-1]
    else:
        hidden, cell = refs[start : start + 2]

    def taken(first):
        convolve(rows_in, w_conv, b_conv, conv)
        target = hidden if first else spare
        gate_step(conv, None, w_input, w_state, b_gates, hidden, cell, target, None, first)
        if not first:
            hidden[...] = spare[...]

    for device in on_first:

        @pl.when(me == device)
        def _():
            taken(True)

    if on_later is not None:

        @pl.when(me >= on_later)
        def _():
            taken(False)

    if on_own is None:
        return
    width = w_state.shape[0]

    def sent(part):
        return pltpu.make_async_copy(
            spare.at[:, part], out.at[0, :, part], sems.at[part.start * 2 // width]
        )

    def last(first):
        gate_step(
            conv,
            pre,
            w_input,
            w_state,
            b_gates,
            hidden,
            cell,
            spare,
            lambda part: sent(part).start(),
            first,
        )

    @pl.when(me == 0)
    def _():
        last(True)

    @pl.when(me > 0)
    def _():
        last(False)

    for low in range(0, width, width // 2):
        sent(slice(low, low + width // 2)).wait()


def step(on_first, on_later, on_own, rows_in, weights, pre, state, name):
    rows = rows_in.shape[0]
    depth, gates = weights[2].shape
    width = gates // 4
    shape = jax.ShapeDtypeStruct
    operands = [rows_in, *weights]
    if on_own is not None:
        operands.append(pre)
    outs = [shape((rows, width), BF16), shape((rows, width), F32)]
    out_specs = [VMEM, VMEM]
    scratch = [pltpu.VMEM((rows, depth), BF16), pltpu.VMEM((rows, width), BF16)]
    aliases = {}
    if on_own is not None:
        outs = [shape((1, rows, width), BF16)] + outs
        out_specs = [HBM] + out_specs
        scratch.append(pltpu.SemaphoreType.DMA((2,)))
    if state is not None:
        skip = len(outs) - 2
        aliases = {len(operands): skip, len(operands) + 1: skip + 1}
        operands += state
    return pl.pallas_call(
        functools.partial(step_kernel, on_first, on_later, on_own, state is not None),
        out_shape=outs,
        in_specs=[VMEM] * len(operands),
        out_specs=out_specs,
        scratch_shapes=scratch,
        input_output_aliases=aliases,
        compiler_params=pltpu.CompilerParams(vmem_limit_bytes=GRANT),
        cost_estimate=pl.CostEstimate(
            flops=2 * rows * (depth + width) * gates,
            transcendentals=5 * rows * width,
            bytes_accessed=rows * width * 8,
        ),
        name=name,
    )(*operands)


def shards(
    features,
    adjacency_tiles,
    src_block,
    dst_block,
    block_count,
    w_conv,
    b_conv,
    w_input,
    w_state,
    b_gates,
):
    owners = lax.axis_size("vert")
    snaps = lax.axis_size("snap")
    last = snaps - 1
    left = lax.ppermute(features[0], "vert", [(i, i + 1) for i in range(owners - 1)])
    right = lax.ppermute(features[0], "vert", [(i + 1, i) for i in range(owners - 1)])
    own, tiles, w_conv, b_conv, w_input, w_state, b_gates = load(
        [features[0], adjacency_tiles[0], w_conv, b_conv[None], w_input, w_state, b_gates[None]]
    )
    lists = [
        pltpu.with_memory_space_constraint(array, pltpu.HBM)
        for array in (src_block, dst_block)
    ]
    whole = aggregate(own, left, right, tiles, *lists, block_count)
    weights = [w_conv, b_conv, w_input, w_state, b_gates]

    handed = snaps >= 3
    arrived = {}
    for hop in range(last, 0, -1):
        routes = [(i, i + hop) for i in range(snaps - hop)]
        if handed and hop == last - 1:
            routes = routes[1:]
        arrived[hop] = lax.ppermute(whole, "snap", routes)
    if handed:
        passed_back = lax.ppermute(arrived[last], "snap", [(last, last - 1)])
    pre = pregate(whole, w_conv, b_conv, w_input)

    state = None
    for stage in range(1, last):
        hop = snaps - stage
        on_first = [] if stage == 2 else [hop]
        on_later = None if stage == 1 else hop + 1
        state = step(on_first, on_later, None, arrived[hop], weights, None, state, "step")
        if stage == min(2, last - 1):
            state = step([last - 1], None, None, passed_back, weights, None, state, "step_back")
    on_first = [1] if snaps == 2 or snaps > 3 else []
    on_later = 2 if handed else None
    rows_in = arrived[1] if snaps > 1 else whole
    return step(on_first, on_later, True, rows_in, weights, pre, state, "step_last")[0]


def solution(mesh):
    placed = (
        P("snap", "vert", None),
        P("snap", "vert", None, None),
        P("snap", "vert"),
        P("snap", "vert"),
        P("snap", "vert"),
        P(),
        P(),
        P(),
        P(),
        P(),
    )
    return jax.shard_map(
        shards, mesh=mesh, in_specs=placed, out_specs=P("snap", "vert", None), check_vma=False
    )
```

```python
import functools

import jax
import jax.numpy as jnp
from jax import lax
from jax.experimental import pallas as pl
from jax.experimental.pallas import tpu as pltpu
from jax.sharding import PartitionSpec as P


forget_bias = 2.0
BF16 = jnp.bfloat16
F32 = jnp.float32
VMEM = pl.BlockSpec(memory_space=pltpu.VMEM)
SMEM = pl.BlockSpec(memory_space=pltpu.SMEM)
HBM = pl.BlockSpec(memory_space=pltpu.HBM)
GRANT = 24 << 20
PARTS = 2


def load_kernel(total, *refs):
    sems = refs[-1]
    copies = []
    for place in range(total):
        copies.append(
            pltpu.make_async_copy(refs[place], refs[total + place], sems.at[place])
        )
    for copy in copies:
        copy.start()
    for copy in copies:
        copy.wait()


def load(arrays):
    bytes_moved = sum(array.size * array.dtype.itemsize for array in arrays)
    return pl.pallas_call(
        functools.partial(load_kernel, len(arrays)),
        out_shape=[jax.ShapeDtypeStruct(array.shape, array.dtype) for array in arrays],
        in_specs=[HBM] * len(arrays),
        out_specs=[VMEM] * len(arrays),
        scratch_shapes=[pltpu.SemaphoreType.DMA((len(arrays),))],
        compiler_params=pltpu.CompilerParams(vmem_limit_bytes=GRANT),
        cost_estimate=pl.CostEstimate(
            flops=0, transcendentals=0, bytes_accessed=2 * bytes_moved
        ),
        name="load",
    )(*(pltpu.with_memory_space_constraint(array, pltpu.HBM) for array in arrays))


def aggregate_kernel(
    parts, own, left, right, tiles, src_in, dst_in, count, *refs
):
    pieces = refs[:parts]
    window, total, src, dst, sems = refs[parts:]
    lists = ((src_in, src), (dst_in, dst))
    copies = [pltpu.make_async_copy(a, b, sems.at[i]) for i, (a, b) in enumerate(lists)]
    for copy in copies:
        copy.start()
    rows = own.shape[0]
    block = tiles.shape[1]
    slots = tiles.shape[0]
    row_blocks = rows // block
    base = (lax.axis_index("vert") - 1) * row_blocks
    window[0:rows] = left[...]
    window[rows : 2 * rows] = own[...]
    window[2 * rows : 3 * rows] = right[...]
    total[...] = jnp.zeros_like(total)
    for copy in copies:
        copy.wait()
    products = []
    for slot in range(slots):
        column = jnp.clip(src[0, slot] - base, 0, 3 * row_blocks - 1)
        start = pl.multiple_of(column * block, block)
        products.append(
            jnp.dot(tiles[slot], window[pl.ds(start, block)], preferred_element_type=F32)
        )
    for slot in range(slots):
        start = pl.multiple_of(jnp.clip(dst[0, slot], 0, row_blocks - 1) * block, block)
        alive = slot < count[0, 0]
        total[pl.ds(start, block)] += jnp.where(alive, products[slot], 0.0)
    share = rows // parts
    for part, piece in enumerate(pieces):
        piece[...] = total[part * share : (part + 1) * share].astype(BF16)


def aggregate(parts, own, left, right, tiles, src, dst, count):
    rows, width = own.shape
    return pl.pallas_call(
        functools.partial(aggregate_kernel, parts),
        out_shape=[jax.ShapeDtypeStruct((rows // parts, width), BF16)] * parts,
        in_specs=[VMEM] * 4 + [HBM] * 2 + [SMEM],
        out_specs=[VMEM] * parts,
        scratch_shapes=[
            pltpu.VMEM((3 * rows, width), BF16),
            pltpu.VMEM((rows, width), F32),
            *(pltpu.SMEM(array.shape, jnp.int32) for array in (src, dst)),
            pltpu.SemaphoreType.DMA((2,)),
        ],
        compiler_params=pltpu.CompilerParams(vmem_limit_bytes=GRANT),
        name="aggregate",
    )(own, left, right, tiles, src, dst, count)


def convolve(rows_in, w_conv, b_conv, conv):
    reached = jnp.dot(rows_in[...], w_conv[...], preferred_element_type=F32) + b_conv[...]
    conv[...] = jnp.maximum(reached, 0.0).astype(BF16)


def pregate_kernel(rows_in, w_conv, b_conv, w_input, *refs):
    pre, _, conv = refs[-3:]
    convolve(rows_in, w_conv, b_conv, conv)
    width = w_input.shape[1] // 4
    for gate in range(4):
        part = slice(gate * width, (gate + 1) * width)
        pre[:, part] = jnp.dot(conv[...], w_input[:, part], preferred_element_type=F32)


def pregate(rows_in, w_conv, b_conv, w_input, out):
    rows = rows_in.shape[0]
    depth, gates = w_input.shape
    operands = [rows_in, w_conv, b_conv, w_input]
    fresh = isinstance(out, tuple)
    return pl.pallas_call(
        pregate_kernel,
        out_shape=[
            jax.ShapeDtypeStruct((rows, gates), F32),
            jax.ShapeDtypeStruct(out if fresh else out.shape, BF16),
        ],
        in_specs=[VMEM] * 4 + ([] if fresh else [HBM]),
        out_specs=[VMEM, HBM],
        scratch_shapes=[pltpu.VMEM((rows, depth), BF16)],
        input_output_aliases={} if fresh else {4: 1},
        compiler_params=pltpu.CompilerParams(vmem_limit_bytes=GRANT),
        cost_estimate=pl.CostEstimate(
            flops=2 * rows * depth * gates, transcendentals=0, bytes_accessed=rows * gates * 4
        ),
        name="pregate",
    )(*operands, *([] if fresh else [out]))


def gate_step(conv, pre, w_input, w_state, b_gates, hidden, cell, fresh_hidden, done, first):
    width = w_state.shape[0]
    chunk = width // 2
    for low in range(0, width, chunk):
        gates = []
        for gate in range(4):
            part = slice(gate * width + low, gate * width + low + chunk)
            if pre is None:
                value = jnp.dot(conv[...], w_input[:, part], preferred_element_type=F32)
            else:
                value = pre[:, part]
            if not first:
                value += jnp.dot(hidden[...], w_state[:, part], preferred_element_type=F32)
            bias = b_gates[:, part]
            if gate == 1:
                bias = bias + forget_bias
            gates.append(value + bias)
        part = slice(low, low + chunk)
        fresh = (0.5 * jnp.tanh(0.5 * gates[0]) + 0.5) * jnp.tanh(gates[2])
        if not first:
            fresh += (0.5 * jnp.tanh(0.5 * gates[1]) + 0.5) * cell[:, part]
        cell[:, part] = fresh
        shown = (0.5 * jnp.tanh(0.5 * gates[3]) + 0.5) * jnp.tanh(fresh)
        fresh_hidden[:, part] = shown.astype(BF16)
        if done is not None:
            done(part)


def step_kernel(on_first, on_later, offset, inputs, *refs):
    rows_in, w_conv, b_conv, w_input, w_state, b_gates = refs[:6]
    ending = offset is not None
    me = lax.axis_index("snap")
    out, hidden, cell, conv, spare = refs[inputs : inputs + 5]
    if ending:
        pre, sems = refs[7], refs[-1]

    def taken(first):
        convolve(rows_in, w_conv, b_conv, conv)
        target = hidden if first else spare
        gate_step(conv, None, w_input, w_state, b_gates, hidden, cell, target, None, first)
        if not first:
            hidden[...] = spare[...]

    for device in on_first:

        @pl.when(me == device)
        def _():
            taken(True)

    if on_later is not None:

        @pl.when(me >= on_later)
        def _():
            taken(False)

    if not ending:
        return
    rows, width = spare.shape

    def sent(part):
        return pltpu.make_async_copy(
            spare.at[:, part],
            out.at[0, offset : offset + rows, part],
            sems.at[part.start * 2 // width],
        )

    def last(first):
        gate_step(
            conv,
            pre,
            w_input,
            w_state,
            b_gates,
            hidden,
            cell,
            spare,
            lambda part: sent(part).start(),
            first,
        )

    @pl.when(me == 0)
    def _():
        last(True)

    @pl.when(me > 0)
    def _():
        last(False)

    for low in range(0, width, width // 2):
        sent(slice(low, low + width // 2)).wait()


def step(on_first, on_later, rows_in, weights, out, state, pre=None, offset=None):
    rows = rows_in.shape[0]
    depth, gates = weights[2].shape
    width = gates // 4
    shape = jax.ShapeDtypeStruct
    operands = [rows_in, *weights, out]
    specs = [VMEM] * 6 + [HBM]
    outs = [shape(out.shape, BF16), shape((rows, width), BF16), shape((rows, width), F32)]
    scratch = [pltpu.VMEM((rows, depth), BF16), pltpu.VMEM((rows, width), BF16)]
    aliases = {6: 0}
    if offset is not None:
        operands.append(pre)
        specs.append(VMEM)
        scratch.append(pltpu.SemaphoreType.DMA((2,)))
    if state is not None:
        for place, array in enumerate(state):
            aliases[len(operands)] = 1 + place
            operands.append(array)
            specs.append(VMEM)
    return pl.pallas_call(
        functools.partial(step_kernel, on_first, on_later, offset, len(operands)),
        out_shape=outs,
        in_specs=specs,
        out_specs=[HBM, VMEM, VMEM],
        scratch_shapes=scratch,
        input_output_aliases=aliases,
        compiler_params=pltpu.CompilerParams(vmem_limit_bytes=GRANT),
        cost_estimate=pl.CostEstimate(
            flops=2 * rows * (depth + width) * gates,
            transcendentals=5 * rows * width,
            bytes_accessed=rows * width * 8,
        ),
    )(*operands)


def shards(
    features,
    adjacency_tiles,
    src_block,
    dst_block,
    block_count,
    w_conv,
    b_conv,
    w_input,
    w_state,
    b_gates,
):
    owners = lax.axis_size("vert")
    snaps = lax.axis_size("snap")
    last = snaps - 1
    left = lax.ppermute(features[0], "vert", [(i, i + 1) for i in range(owners - 1)])
    right = lax.ppermute(features[0], "vert", [(i + 1, i) for i in range(owners - 1)])
    own, tiles, w_conv, b_conv, w_input, w_state, b_gates = load(
        [features[0], adjacency_tiles[0], w_conv, b_conv[None], w_input, w_state, b_gates[None]]
    )
    lists = [
        pltpu.with_memory_space_constraint(array, pltpu.HBM)
        for array in (src_block, dst_block)
    ]
    halves = aggregate(PARTS, own, left, right, tiles, *lists, block_count)
    weights = [w_conv, b_conv, w_input, w_state, b_gates]
    handed = snaps >= 3

    def shifted(part, hop):
        routes = [(i, i + hop) for i in range(snaps - hop)]
        if handed and hop == last - 1:
            routes = routes[1:]
        return lax.ppermute(halves[part], "snap", routes)

    arrived = {(hop, part): shifted(part, hop) for hop, part in sends(snaps)}
    out = (1, own.shape[0], w_state.shape[0])
    share = own.shape[0] // PARTS
    pre = {}
    for part in range(PARTS):
        pre[part], out = pregate(halves[part], w_conv, b_conv, w_input, out)
    passed_back = {}
    states = {part: None for part in range(PARTS)}

    def advance(part, stage):
        hop = snaps - stage
        on_first = [] if stage == 2 else [hop]
        on_later = None if stage == 1 else hop + 1
        out_now, *state = step(on_first, on_later, arrived[hop, part], weights, out, states[part])
        states[part] = state
        return out_now

    def receive_back(part):
        out_now, *state = step([last - 1], None, passed_back[part], weights, out, states[part])
        states[part] = state
        return out_now

    if handed:
        for part in range(PARTS):
            passed_back[part] = lax.ppermute(
                arrived[last, part], "snap", [(last, last - 1)]
            )
            out = advance(part, 1) if snaps > 3 else out
    for part in range(PARTS):
        if snaps == 3:
            out = advance(part, 1)
        for stage in range(2, last):
            out = advance(part, stage)
            if stage == 2:
                out = receive_back(part)
        if snaps == 3:
            out = receive_back(part)
        on_first = [1] if snaps == 2 or snaps > 3 else []
        on_later = 2 if handed else None
        rows_in = arrived[1, part] if snaps > 1 else halves[part]
        out = step(
            on_first, on_later, rows_in, weights, out, states[part], pre[part], part * share
        )[0]
    return out


def sends(snaps):
    order = [(snaps - 1, part) for part in range(PARTS)] if snaps > 1 else []
    return order + [(hop, part) for part in range(PARTS) for hop in range(snaps - 2, 0, -1)]


def solution(mesh):
    placed = (
        P("snap", "vert", None),
        P("snap", "vert", None, None),
        P("snap", "vert"),
        P("snap", "vert"),
        P("snap", "vert"),
        P(),
        P(),
        P(),
        P(),
        P(),
    )

    return jax.shard_map(
        shards, mesh=mesh, in_specs=placed, out_specs=P("snap", "vert", None), check_vma=False
    )
```

```python
import functools

import jax
import jax.numpy as jnp
from jax import lax
from jax.experimental import pallas as pl
from jax.experimental.pallas import tpu as pltpu
from jax.sharding import PartitionSpec as P


forget_bias = 2.0
BF16 = jnp.bfloat16
F32 = jnp.float32
VMEM = pl.BlockSpec(memory_space=pltpu.VMEM)
SMEM = pl.BlockSpec(memory_space=pltpu.SMEM)
HBM = pl.BlockSpec(memory_space=pltpu.HBM)
GRANT = 24 << 20
PARTS = 1
LAST_BLOCKS = 4


def load_kernel(total, *refs):
    sems = refs[-1]
    copies = []
    for place in range(total):
        copies.append(
            pltpu.make_async_copy(refs[place], refs[total + place], sems.at[place])
        )
    for copy in copies:
        copy.start()
    for copy in copies:
        copy.wait()


def load(arrays):
    bytes_moved = sum(array.size * array.dtype.itemsize for array in arrays)
    return pl.pallas_call(
        functools.partial(load_kernel, len(arrays)),
        out_shape=[jax.ShapeDtypeStruct(array.shape, array.dtype) for array in arrays],
        in_specs=[HBM] * len(arrays),
        out_specs=[VMEM] * len(arrays),
        scratch_shapes=[pltpu.SemaphoreType.DMA((len(arrays),))],
        compiler_params=pltpu.CompilerParams(vmem_limit_bytes=GRANT),
        cost_estimate=pl.CostEstimate(
            flops=0, transcendentals=0, bytes_accessed=2 * bytes_moved
        ),
        name="load",
    )(*(pltpu.with_memory_space_constraint(array, pltpu.HBM) for array in arrays))


def aggregate_kernel(
    parts, own, left, right, tiles, src_in, dst_in, count, *refs
):
    pieces = refs[:parts]
    window, total, src, dst, sems = refs[parts:]
    lists = ((src_in, src), (dst_in, dst))
    copies = [pltpu.make_async_copy(a, b, sems.at[i]) for i, (a, b) in enumerate(lists)]
    for copy in copies:
        copy.start()
    rows = own.shape[0]
    block = tiles.shape[1]
    slots = tiles.shape[0]
    row_blocks = rows // block
    base = (lax.axis_index("vert") - 1) * row_blocks
    window[0:rows] = left[...]
    window[rows : 2 * rows] = own[...]
    window[2 * rows : 3 * rows] = right[...]
    total[...] = jnp.zeros_like(total)
    for copy in copies:
        copy.wait()
    products = []
    for slot in range(slots):
        column = jnp.clip(src[0, slot] - base, 0, 3 * row_blocks - 1)
        start = pl.multiple_of(column * block, block)
        products.append(
            jnp.dot(tiles[slot], window[pl.ds(start, block)], preferred_element_type=F32)
        )
    for slot in range(slots):
        start = pl.multiple_of(jnp.clip(dst[0, slot], 0, row_blocks - 1) * block, block)
        alive = slot < count[0, 0]
        total[pl.ds(start, block)] += jnp.where(alive, products[slot], 0.0)
    share = rows // parts
    for part, piece in enumerate(pieces):
        piece[...] = total[part * share : (part + 1) * share].astype(BF16)


def aggregate(parts, own, left, right, tiles, src, dst, count):
    rows, width = own.shape
    return pl.pallas_call(
        functools.partial(aggregate_kernel, parts),
        out_shape=[jax.ShapeDtypeStruct((rows // parts, width), BF16)] * parts,
        in_specs=[VMEM] * 4 + [HBM] * 2 + [SMEM],
        out_specs=[VMEM] * parts,
        scratch_shapes=[
            pltpu.VMEM((3 * rows, width), BF16),
            pltpu.VMEM((rows, width), F32),
            *(pltpu.SMEM(array.shape, jnp.int32) for array in (src, dst)),
            pltpu.SemaphoreType.DMA((2,)),
        ],
        compiler_params=pltpu.CompilerParams(vmem_limit_bytes=GRANT),
        name="aggregate",
    )(own, left, right, tiles, src, dst, count)


def convolve(rows_in, w_conv, b_conv, conv):
    reached = jnp.dot(rows_in[...], w_conv[...], preferred_element_type=F32) + b_conv[...]
    conv[...] = jnp.maximum(reached, 0.0).astype(BF16)


def bias_of(b_gates, gate, part):
    return b_gates[:, part] + (forget_bias if gate == 1 else 0.0)


def pregate_kernel(only, rows_in, w_conv, b_conv, w_input, b_gates, *refs):
    pre, _, conv = refs[-3:]
    width = w_input.shape[1] // 4

    def run():
        convolve(rows_in, w_conv, b_conv, conv)
        for gate in range(4):
            part = slice(gate * width, (gate + 1) * width)
            pre[:, part] = jnp.dot(
                conv[...], w_input[:, part], preferred_element_type=F32
            ) + bias_of(b_gates, gate, part)

    if only is None:
        run()
    else:
        pl.when(lax.axis_index("snap") == only)(run)


def pregate(only, rows_in, w_conv, b_conv, w_input, b_gates, out):
    rows = rows_in.shape[0]
    depth, gates = w_input.shape
    fresh = isinstance(out, tuple)
    return pl.pallas_call(
        functools.partial(pregate_kernel, only),
        out_shape=[
            jax.ShapeDtypeStruct((rows, gates), F32),
            jax.ShapeDtypeStruct(out if fresh else out.shape, BF16),
        ],
        in_specs=[VMEM] * 5 + ([] if fresh else [HBM]),
        out_specs=[VMEM, HBM],
        scratch_shapes=[pltpu.VMEM((rows, depth), BF16)],
        input_output_aliases={} if fresh else {5: 1},
        compiler_params=pltpu.CompilerParams(vmem_limit_bytes=GRANT),
        cost_estimate=pl.CostEstimate(
            flops=2 * rows * depth * gates, transcendentals=0, bytes_accessed=rows * gates * 4
        ),
        name="pregate",
    )(rows_in, w_conv, b_conv, w_input, b_gates, *([] if fresh else [out]))


def gate_step(inner, pre, w_input, w_state, b_gates, hidden, cell, target, rows, store_cell=True):
    width = w_state.shape[0]
    chunk = width // 2
    for low in range(0, width, chunk):
        gates = []
        for gate in range(4):
            part = slice(gate * width + low, gate * width + low + chunk)
            if pre is None:
                value = jnp.dot(inner[rows], w_input[:, part], preferred_element_type=F32)
            else:
                value = pre[rows, part]
            if hidden is not None:
                value += jnp.dot(hidden[rows], w_state[:, part], preferred_element_type=F32)
            if pre is None:
                value += bias_of(b_gates, gate, part)
            gates.append(value)
        part = slice(low, low + chunk)
        fresh = (0.5 * jnp.tanh(0.5 * gates[0]) + 0.5) * jnp.tanh(gates[2])
        if hidden is not None:
            fresh += (0.5 * jnp.tanh(0.5 * gates[1]) + 0.5) * cell[rows, part]
        if store_cell:
            cell[rows, part] = fresh
        shown = (0.5 * jnp.tanh(0.5 * gates[3]) + 0.5) * jnp.tanh(fresh)
        target[rows, part] = shown.astype(BF16)


def step_kernel(on_first, on_later, inputs, *refs):
    rows_in, w_conv, b_conv, w_input, w_state, b_gates = refs[:6]
    before = refs[7] if inputs > 7 else None
    _, hidden, cell, conv = refs[inputs:]
    me = lax.axis_index("snap")
    every = slice(None)

    def taken(first):
        convolve(rows_in, w_conv, b_conv, conv)
        source = None if first else before
        gate_step(conv, None, w_input, w_state, b_gates, source, cell, hidden, every)

    for device in on_first:
        pl.when(me == device)(functools.partial(taken, True))
    if on_later is not None:
        pl.when(me >= on_later)(functools.partial(taken, False))


def step(on_first, on_later, rows_in, weights, out, state):
    rows = rows_in.shape[0]
    depth, gates = weights[2].shape
    width = gates // 4
    shape = jax.ShapeDtypeStruct
    operands = [rows_in, *weights, out]
    aliases = {6: 0}
    if state is not None:
        aliases[8] = 2
        if on_later is None:
            aliases[7] = 1
        operands += state
    return pl.pallas_call(
        functools.partial(step_kernel, on_first, on_later, len(operands)),
        out_shape=[shape(out.shape, BF16), shape((rows, width), BF16), shape((rows, width), F32)],
        in_specs=[VMEM] * 6 + [HBM] + [VMEM] * (len(operands) - 7),
        out_specs=[HBM, VMEM, VMEM],
        scratch_shapes=[pltpu.VMEM((rows, depth), BF16)],
        input_output_aliases=aliases,
        compiler_params=pltpu.CompilerParams(vmem_limit_bytes=GRANT),
        cost_estimate=pl.CostEstimate(
            flops=2 * rows * (depth + width) * gates,
            transcendentals=5 * rows * width,
            bytes_accessed=rows * width * 8,
        ),
    )(*operands)


def finish_kernel(snaps, offset, *refs):
    rows_in, w_conv, b_conv, w_input, w_state, b_gates, _, pre = refs[:8]
    out, cell, conv, middle, shown, sems = refs[-6:]
    before = refs[8] if snaps >= 3 else None
    prepared = refs[10] if snaps > 3 else None
    me = lax.axis_index("snap")
    rows = shown.shape[0]
    every = slice(None)

    def taken(first, ready):
        if ready is None:
            convolve(rows_in, w_conv, b_conv, conv)
        source = None if first else before
        gate_step(conv, ready, w_input, w_state, b_gates, source, cell, middle, every)

    if snaps == 3:

        @pl.when(me == 1)
        def _():
            middle[...] = before[...]

    if snaps == 2 or snaps > 3:
        pl.when(me == 1)(functools.partial(taken, True, None))
    if snaps > 3:
        pl.when(me == snaps - 2)(functools.partial(taken, False, prepared))
        pl.when((me > 1) & (me != snaps - 2))(functools.partial(taken, False, None))
    elif snaps == 3:
        pl.when(me == 2)(functools.partial(taken, False, None))

    blocks = LAST_BLOCKS if rows % (16 * LAST_BLOCKS) == 0 else 1
    share = rows // blocks

    def sent(block):
        start = block * share
        return pltpu.make_async_copy(
            shown.at[start : start + share],
            out.at[0, offset + start : offset + start + share],
            sems.at[block],
        )

    def last(first):
        source = None if first else middle
        for block in range(blocks):
            part = slice(block * share, (block + 1) * share)
            gate_step(None, pre, w_input, w_state, b_gates, source, cell, shown, part, False)
            sent(block).start()

    pl.when(me == 0)(functools.partial(last, True))
    pl.when(me > 0)(functools.partial(last, False))
    for block in range(blocks):
        sent(block).wait()


def finish(snaps, offset, rows_in, weights, out, pre, state, prepared):
    rows = rows_in.shape[0]
    depth, gates = weights[2].shape
    width = gates // 4
    shape = jax.ShapeDtypeStruct
    operands = [rows_in, *weights, out, pre]
    aliases = {6: 0}
    if state is not None:
        aliases[9] = 1
        operands += state
    if prepared is not None:
        operands.append(prepared)
    return pl.pallas_call(
        functools.partial(finish_kernel, snaps, offset),
        out_shape=[shape(out.shape, BF16), shape((rows, width), F32)],
        in_specs=[VMEM] * 6 + [HBM] + [VMEM] * (len(operands) - 7),
        out_specs=[HBM, VMEM],
        scratch_shapes=[
            pltpu.VMEM((rows, depth), BF16),
            pltpu.VMEM((rows, width), BF16),
            pltpu.VMEM((rows, width), BF16),
            pltpu.SemaphoreType.DMA((LAST_BLOCKS,)),
        ],
        input_output_aliases=aliases,
        compiler_params=pltpu.CompilerParams(vmem_limit_bytes=GRANT),
        cost_estimate=pl.CostEstimate(
            flops=2 * rows * (depth + 2 * width) * gates,
            transcendentals=10 * rows * width,
            bytes_accessed=rows * width * 8,
        ),
        name="finish",
    )(*operands)[0]


def shards(
    features,
    adjacency_tiles,
    src_block,
    dst_block,
    block_count,
    w_conv,
    b_conv,
    w_input,
    w_state,
    b_gates,
):
    owners = lax.axis_size("vert")
    snaps = lax.axis_size("snap")
    last = snaps - 1
    left = lax.ppermute(features[0], "vert", [(i, i + 1) for i in range(owners - 1)])
    right = lax.ppermute(features[0], "vert", [(i + 1, i) for i in range(owners - 1)])
    own, tiles, w_conv, b_conv, w_input, w_state, b_gates = load(
        [features[0], adjacency_tiles[0], w_conv, b_conv[None], w_input, w_state, b_gates[None]]
    )
    lists = [
        pltpu.with_memory_space_constraint(array, pltpu.HBM)
        for array in (src_block, dst_block)
    ]
    halves = aggregate(PARTS, own, left, right, tiles, *lists, block_count)
    weights = [w_conv, b_conv, w_input, w_state, b_gates]
    handed = snaps >= 3

    def shifted(part, hop):
        routes = [(i, i + hop) for i in range(snaps - hop)]
        if handed and hop == last - 1:
            routes = routes[1:]
        return lax.ppermute(halves[part], "snap", routes)

    arrived = {(hop, part): shifted(part, hop) for hop, part in sends(snaps)}
    out = (1, own.shape[0], w_state.shape[0])
    share = own.shape[0] // PARTS
    pre = {}
    for part in range(PARTS):
        pre[part], out = pregate(None, halves[part], w_conv, b_conv, w_input, b_gates, out)
    passed_back = {}
    states = {part: None for part in range(PARTS)}

    def advance(part, stage):
        hop = snaps - stage
        on_first = [] if stage == 2 else [hop]
        on_later = None if stage == 1 else hop + 1
        out_now, *state = step(on_first, on_later, arrived[hop, part], weights, out, states[part])
        states[part] = state
        return out_now

    prepared = {part: None for part in range(PARTS)}

    def prepare(part):
        prepared[part], out_now = pregate(
            last - 1, arrived[1, part], w_conv, b_conv, w_input, b_gates, out
        )
        return out_now

    def receive_back(part):
        out_now, *state = step([last - 1], None, passed_back[part], weights, out, states[part])
        states[part] = state
        return out_now

    if handed:
        for part in range(PARTS):
            passed_back[part] = lax.ppermute(
                arrived[last, part], "snap", [(last, last - 1)]
            )
            out = advance(part, 1) if snaps > 3 else out
    for part in range(PARTS):
        if snaps == 3:
            out = advance(part, 1)
        for stage in range(2, last):
            out = advance(part, stage)
            if stage == 2:
                out = prepare(part)
                out = receive_back(part)
        if snaps == 3:
            out = receive_back(part)
        rows_in = arrived[1, part] if snaps > 1 else halves[part]
        out = finish(
            snaps, part * share, rows_in, weights, out, pre[part], states[part], prepared[part]
        )
    return out


def sends(snaps):
    order = [(snaps - 1, part) for part in range(PARTS)] if snaps > 1 else []
    return order + [(hop, part) for part in range(PARTS) for hop in range(snaps - 2, 0, -1)]


def solution(mesh):
    placed = (
        P("snap", "vert", None),
        P("snap", "vert", None, None),
        P("snap", "vert"),
        P("snap", "vert"),
        P("snap", "vert"),
        P(),
        P(),
        P(),
        P(),
        P(),
    )

    return jax.shard_map(
        shards, mesh=mesh, in_specs=placed, out_specs=P("snap", "vert", None), check_vma=False
    )
```

```python
import functools

import jax
import jax.numpy as jnp
from jax import lax
from jax.experimental import pallas as pl
from jax.experimental.pallas import tpu as pltpu
from jax.sharding import PartitionSpec as P


forget_bias = 2.0
BF16 = jnp.bfloat16
F32 = jnp.float32
VMEM = pl.BlockSpec(memory_space=pltpu.VMEM)
SMEM = pl.BlockSpec(memory_space=pltpu.SMEM)
HBM = pl.BlockSpec(memory_space=pltpu.HBM)
GRANT = 24 << 20
PARTS = 1
LAST_BLOCKS = 4


def load_kernel(total, *refs):
    sems = refs[-1]
    copies = []
    for place in range(total):
        copies.append(
            pltpu.make_async_copy(refs[place], refs[total + place], sems.at[place])
        )
    for copy in copies:
        copy.start()
    for copy in copies:
        copy.wait()


def load(arrays):
    bytes_moved = sum(array.size * array.dtype.itemsize for array in arrays)
    return pl.pallas_call(
        functools.partial(load_kernel, len(arrays)),
        out_shape=[jax.ShapeDtypeStruct(array.shape, array.dtype) for array in arrays],
        in_specs=[HBM] * len(arrays),
        out_specs=[VMEM] * len(arrays),
        scratch_shapes=[pltpu.SemaphoreType.DMA((len(arrays),))],
        compiler_params=pltpu.CompilerParams(vmem_limit_bytes=GRANT),
        cost_estimate=pl.CostEstimate(
            flops=0, transcendentals=0, bytes_accessed=2 * bytes_moved
        ),
        name="load",
    )(*(pltpu.with_memory_space_constraint(array, pltpu.HBM) for array in arrays))


def aggregate_kernel(
    parts, own, outer, inner, tiles, src_in, dst_in, count, *refs
):
    pieces = refs[:parts]
    window, total, src, dst, sems = refs[parts:]
    lists = ((src_in, src), (dst_in, dst))
    copies = [pltpu.make_async_copy(a, b, sems.at[i]) for i, (a, b) in enumerate(lists)]
    for copy in copies:
        copy.start()
    rows = own.shape[0]
    block = tiles.shape[1]
    slots = tiles.shape[0]
    row_blocks = rows // block
    base = (lax.axis_index("vert") - 1) * row_blocks
    window[rows : 2 * rows] = own[...]
    side = lax.axis_index("vert") % 2

    @pl.when(side == 0)
    def _():
        window[0:rows] = outer[...]
        window[2 * rows : 3 * rows] = inner[...]

    @pl.when(side == 1)
    def _():
        window[0:rows] = inner[...]
        window[2 * rows : 3 * rows] = outer[...]

    total[...] = jnp.zeros_like(total)
    for copy in copies:
        copy.wait()
    products = []
    for slot in range(slots):
        column = jnp.clip(src[0, slot] - base, 0, 3 * row_blocks - 1)
        start = pl.multiple_of(column * block, block)
        products.append(
            jnp.dot(tiles[slot], window[pl.ds(start, block)], preferred_element_type=F32)
        )
    for slot in range(slots):
        start = pl.multiple_of(jnp.clip(dst[0, slot], 0, row_blocks - 1) * block, block)
        alive = slot < count[0, 0]
        total[pl.ds(start, block)] += jnp.where(alive, products[slot], 0.0)
    share = rows // parts
    for part, piece in enumerate(pieces):
        piece[...] = total[part * share : (part + 1) * share].astype(BF16)


def aggregate(parts, own, outer, inner, tiles, src, dst, count):
    rows, width = own.shape
    return pl.pallas_call(
        functools.partial(aggregate_kernel, parts),
        out_shape=[jax.ShapeDtypeStruct((rows // parts, width), BF16)] * parts,
        in_specs=[VMEM] * 4 + [HBM] * 2 + [SMEM],
        out_specs=[VMEM] * parts,
        scratch_shapes=[
            pltpu.VMEM((3 * rows, width), BF16),
            pltpu.VMEM((rows, width), F32),
            *(pltpu.SMEM(array.shape, jnp.int32) for array in (src, dst)),
            pltpu.SemaphoreType.DMA((2,)),
        ],
        compiler_params=pltpu.CompilerParams(vmem_limit_bytes=GRANT),
        name="aggregate",
    )(own, outer, inner, tiles, src, dst, count)


def convolve(rows_in, w_conv, b_conv, conv, part=slice(None)):
    reached = jnp.dot(rows_in[part], w_conv[...], preferred_element_type=F32) + b_conv[...]
    conv[part] = jnp.maximum(reached, 0.0).astype(BF16)


def bias_of(b_gates, gate, part):
    return b_gates[:, part] + (forget_bias if gate == 1 else 0.0)


def pregate_kernel(rows_in, w_conv, b_conv, w_input, b_gates, *refs):
    pre, _, conv = refs[-3:]
    width = w_input.shape[1] // 4
    convolve(rows_in, w_conv, b_conv, conv)
    for gate in range(4):
        part = slice(gate * width, (gate + 1) * width)
        pre[:, part] = jnp.dot(
            conv[...], w_input[:, part], preferred_element_type=F32
        ) + bias_of(b_gates, gate, part)


def pregate(rows_in, w_conv, b_conv, w_input, b_gates, out):
    rows = rows_in.shape[0]
    depth, gates = w_input.shape
    fresh = isinstance(out, tuple)
    return pl.pallas_call(
        pregate_kernel,
        out_shape=[
            jax.ShapeDtypeStruct((rows, gates), F32),
            jax.ShapeDtypeStruct(out if fresh else out.shape, BF16),
        ],
        in_specs=[VMEM] * 5 + ([] if fresh else [HBM]),
        out_specs=[VMEM, HBM],
        scratch_shapes=[pltpu.VMEM((rows, depth), BF16)],
        input_output_aliases={} if fresh else {5: 1},
        compiler_params=pltpu.CompilerParams(vmem_limit_bytes=GRANT),
        cost_estimate=pl.CostEstimate(
            flops=2 * rows * depth * gates, transcendentals=0, bytes_accessed=rows * gates * 4
        ),
        name="pregate",
    )(rows_in, w_conv, b_conv, w_input, b_gates, *([] if fresh else [out]))


def gate_step(inner, pre, w_input, w_state, b_gates, hidden, cell, target, rows, store_cell=True):
    width = w_state.shape[0]
    chunk = width // 2
    for low in range(0, width, chunk):
        gates = []
        for gate in range(4):
            part = slice(gate * width + low, gate * width + low + chunk)
            if pre is None:
                value = jnp.dot(inner[rows], w_input[:, part], preferred_element_type=F32)
            else:
                value = pre[rows, part]
            if hidden is not None:
                value += jnp.dot(hidden[rows], w_state[:, part], preferred_element_type=F32)
            if pre is None:
                value += bias_of(b_gates, gate, part)
            gates.append(value)
        part = slice(low, low + chunk)
        fresh = (0.5 * jnp.tanh(0.5 * gates[0]) + 0.5) * jnp.tanh(gates[2])
        if hidden is not None:
            fresh += (0.5 * jnp.tanh(0.5 * gates[1]) + 0.5) * cell[rows, part]
        if store_cell:
            cell[rows, part] = fresh
        shown = (0.5 * jnp.tanh(0.5 * gates[3]) + 0.5) * jnp.tanh(fresh)
        target[rows, part] = shown.astype(BF16)


def step_kernel(on_first, on_later, inputs, *refs):
    rows_in, w_conv, b_conv, w_input, w_state, b_gates = refs[:6]
    before = refs[7] if inputs > 7 else None
    _, hidden, cell, conv = refs[inputs:]
    me = lax.axis_index("snap")
    every = slice(None)

    def taken(first):
        convolve(rows_in, w_conv, b_conv, conv)
        source = None if first else before
        gate_step(conv, None, w_input, w_state, b_gates, source, cell, hidden, every)

    for device in on_first:
        pl.when(me == device)(functools.partial(taken, True))
    if on_later is not None:
        pl.when(me >= on_later)(functools.partial(taken, False))


def step(on_first, on_later, rows_in, weights, out, state):
    rows = rows_in.shape[0]
    depth, gates = weights[2].shape
    width = gates // 4
    shape = jax.ShapeDtypeStruct
    operands = [rows_in, *weights, out]
    aliases = {6: 0}
    if state is not None:
        aliases[8] = 2
        if on_later is None:
            aliases[7] = 1
        operands += state
    return pl.pallas_call(
        functools.partial(step_kernel, on_first, on_later, len(operands)),
        out_shape=[shape(out.shape, BF16), shape((rows, width), BF16), shape((rows, width), F32)],
        in_specs=[VMEM] * 6 + [HBM] + [VMEM] * (len(operands) - 7),
        out_specs=[HBM, VMEM, VMEM],
        scratch_shapes=[pltpu.VMEM((rows, depth), BF16)],
        input_output_aliases=aliases,
        compiler_params=pltpu.CompilerParams(vmem_limit_bytes=GRANT),
        cost_estimate=pl.CostEstimate(
            flops=2 * rows * (depth + width) * gates,
            transcendentals=5 * rows * width,
            bytes_accessed=rows * width * 8,
        ),
    )(*operands)


def finish_kernel(snaps, offset, *refs):
    rows_in, w_conv, b_conv, w_input, w_state, b_gates, _, pre = refs[:8]
    out, cell, conv, middle, shown, sems = refs[-6:]
    before = refs[8] if snaps >= 3 else None
    me = lax.axis_index("snap")
    rows = shown.shape[0]
    blocks = LAST_BLOCKS if rows % (16 * LAST_BLOCKS) == 0 else 1
    share = rows // blocks

    def sent(block):
        start = block * share
        return pltpu.make_async_copy(
            shown.at[start : start + share],
            out.at[0, offset + start : offset + start + share],
            sems.at[block],
        )

    def run(source, begins, carried):
        def taken(part):
            convolve(rows_in, w_conv, b_conv, conv, part)
            gate_step(conv, None, w_input, w_state, b_gates, source, cell, middle, part)

        def last(block, part):
            gate_step(None, pre, w_input, w_state, b_gates, carried, cell, shown, part, False)
            sent(block).start()

        parts = [slice(block * share, (block + 1) * share) for block in range(blocks)]
        if begins:
            taken(parts[0])
        for block, part in enumerate(parts):
            if begins and block + 1 < blocks:
                taken(parts[block + 1])
            last(block, part)

    pl.when(me == 0)(functools.partial(run, None, False, None))
    if snaps > 1:
        middle_now = before if snaps == 3 else middle
        pl.when(me == 1)(functools.partial(run, None, snaps != 3, middle_now))
    if snaps > 2:
        pl.when(me > 1)(functools.partial(run, before, True, middle))
    for block in range(blocks):
        sent(block).wait()


def finish(snaps, offset, rows_in, weights, out, pre, state):
    rows = rows_in.shape[0]
    depth, gates = weights[2].shape
    width = gates // 4
    shape = jax.ShapeDtypeStruct
    operands = [rows_in, *weights, out, pre]
    aliases = {6: 0}
    if state is not None:
        aliases[9] = 1
        operands += state
    return pl.pallas_call(
        functools.partial(finish_kernel, snaps, offset),
        out_shape=[shape(out.shape, BF16), shape((rows, width), F32)],
        in_specs=[VMEM] * 6 + [HBM] + [VMEM] * (len(operands) - 7),
        out_specs=[HBM, VMEM],
        scratch_shapes=[
            pltpu.VMEM((rows, depth), BF16),
            pltpu.VMEM((rows, width), BF16),
            pltpu.VMEM((rows, width), BF16),
            pltpu.SemaphoreType.DMA((LAST_BLOCKS,)),
        ],
        input_output_aliases=aliases,
        compiler_params=pltpu.CompilerParams(vmem_limit_bytes=GRANT),
        cost_estimate=pl.CostEstimate(
            flops=2 * rows * (depth + 2 * width) * gates,
            transcendentals=10 * rows * width,
            bytes_accessed=rows * width * 8,
        ),
        name="finish",
    )(*operands)[0]


def shards(
    features,
    adjacency_tiles,
    src_block,
    dst_block,
    block_count,
    w_conv,
    b_conv,
    w_input,
    w_state,
    b_gates,
):
    owners = lax.axis_size("vert")
    snaps = lax.axis_size("snap")
    last = snaps - 1
    odd = [(i, i + 1) for i in range(1, owners - 1, 2)]
    even = [(i, i + 1) for i in range(0, owners - 1, 2)]
    outer = lax.ppermute(features[0], "vert", odd + [(b, a) for a, b in odd])
    inner = lax.ppermute(features[0], "vert", even + [(b, a) for a, b in even])
    own, tiles = load([features[0], adjacency_tiles[0]])
    lists = [
        pltpu.with_memory_space_constraint(array, pltpu.HBM)
        for array in (src_block, dst_block)
    ]
    halves = aggregate(PARTS, own, outer, inner, tiles, *lists, block_count)
    weights = load([w_conv, b_conv[None], w_input, w_state, b_gates[None]])
    w_conv, b_conv, w_input, w_state, b_gates = weights
    handed = snaps >= 3

    def shifted(part, hop):
        routes = [(i, i + hop) for i in range(snaps - hop)]
        if handed and hop == last - 1:
            routes = routes[1:]
        return lax.ppermute(halves[part], "snap", routes)

    arrived = {(hop, part): shifted(part, hop) for hop, part in sends(snaps)}
    out = (1, own.shape[0], w_state.shape[0])
    share = own.shape[0] // PARTS
    pre = {}
    for part in range(PARTS):
        pre[part], out = pregate(halves[part], w_conv, b_conv, w_input, b_gates, out)
    passed_back = {}
    states = {part: None for part in range(PARTS)}

    def advance(part, stage):
        hop = snaps - stage
        on_first = [] if stage == 2 else [hop]
        on_later = None if stage == 1 else hop + 1
        out_now, *state = step(on_first, on_later, arrived[hop, part], weights, out, states[part])
        states[part] = state
        return out_now

    def receive_back(part):
        out_now, *state = step([last - 1], None, passed_back[part], weights, out, states[part])
        states[part] = state
        return out_now

    if handed:
        for part in range(PARTS):
            passed_back[part] = lax.ppermute(
                arrived[last, part], "snap", [(last, last - 1)]
            )
            out = advance(part, 1) if snaps > 3 else out
    for part in range(PARTS):
        if snaps == 3:
            out = advance(part, 1)
        for stage in range(2, last):
            out = advance(part, stage)
            if stage == 2:
                out = receive_back(part)
        if snaps == 3:
            out = receive_back(part)
        rows_in = arrived[1, part] if snaps > 1 else halves[part]
        out = finish(
            snaps, part * share, rows_in, weights, out, pre[part], states[part]
        )
    return out


def sends(snaps):
    order = [(snaps - 1, part) for part in range(PARTS)] if snaps > 1 else []
    return order + [(hop, part) for part in range(PARTS) for hop in range(snaps - 2, 0, -1)]


def solution(mesh):
    placed = (
        P("snap", "vert", None),
        P("snap", "vert", None, None),
        P("snap", "vert"),
        P("snap", "vert"),
        P("snap", "vert"),
        P(),
        P(),
        P(),
        P(),
        P(),
    )

    return jax.shard_map(
        shards, mesh=mesh, in_specs=placed, out_specs=P("snap", "vert", None), check_vma=False
    )
```

```python
import functools

import jax
import jax.numpy as jnp
from jax import lax
from jax.experimental import pallas as pl
from jax.experimental.pallas import tpu as pltpu
from jax.sharding import PartitionSpec as P


forget_bias = 2.0
BF16 = jnp.bfloat16
F32 = jnp.float32
VMEM = pl.BlockSpec(memory_space=pltpu.VMEM)
SMEM = pl.BlockSpec(memory_space=pltpu.SMEM)
HBM = pl.BlockSpec(memory_space=pltpu.HBM)
GRANT = 24 << 20
PARTS = 1
LAST_BLOCKS = 4


def load_kernel(total, *refs):
    sems = refs[-1]
    copies = []
    for place in range(total):
        copies.append(
            pltpu.make_async_copy(refs[place], refs[total + place], sems.at[place])
        )
    for copy in copies:
        copy.start()
    for copy in copies:
        copy.wait()


def load(arrays):
    bytes_moved = sum(array.size * array.dtype.itemsize for array in arrays)
    return pl.pallas_call(
        functools.partial(load_kernel, len(arrays)),
        out_shape=[jax.ShapeDtypeStruct(array.shape, array.dtype) for array in arrays],
        in_specs=[HBM] * len(arrays),
        out_specs=[VMEM] * len(arrays),
        scratch_shapes=[pltpu.SemaphoreType.DMA((len(arrays),))],
        compiler_params=pltpu.CompilerParams(vmem_limit_bytes=GRANT),
        cost_estimate=pl.CostEstimate(
            flops=0, transcendentals=0, bytes_accessed=2 * bytes_moved
        ),
        name="load",
    )(*(pltpu.with_memory_space_constraint(array, pltpu.HBM) for array in arrays))


def aggregate_kernel(
    parts, own, outer, inner, tiles, src_in, dst_in, count, *refs
):
    pieces = refs[:parts]
    window, total, src, dst, sems = refs[parts:]
    lists = ((src_in, src), (dst_in, dst))
    copies = [pltpu.make_async_copy(a, b, sems.at[i]) for i, (a, b) in enumerate(lists)]
    for copy in copies:
        copy.start()
    rows = own.shape[0]
    block = tiles.shape[1]
    slots = tiles.shape[0]
    row_blocks = rows // block
    base = (lax.axis_index("vert") - 1) * row_blocks
    window[rows : 2 * rows] = own[...]
    side = lax.axis_index("vert") % 2

    @pl.when(side == 0)
    def _():
        window[0:rows] = outer[...]
        window[2 * rows : 3 * rows] = inner[...]

    @pl.when(side == 1)
    def _():
        window[0:rows] = inner[...]
        window[2 * rows : 3 * rows] = outer[...]

    total[...] = jnp.zeros_like(total)
    for copy in copies:
        copy.wait()
    products = []
    for slot in range(slots):
        column = jnp.clip(src[0, slot] - base, 0, 3 * row_blocks - 1)
        start = pl.multiple_of(column * block, block)
        products.append(
            jnp.dot(tiles[slot], window[pl.ds(start, block)], preferred_element_type=F32)
        )
    for slot in range(slots):
        start = pl.multiple_of(jnp.clip(dst[0, slot], 0, row_blocks - 1) * block, block)
        alive = slot < count[0, 0]
        total[pl.ds(start, block)] += jnp.where(alive, products[slot], 0.0)
    share = rows // parts
    for part, piece in enumerate(pieces):
        piece[...] = total[part * share : (part + 1) * share].astype(BF16)


def aggregate(parts, own, outer, inner, tiles, src, dst, count):
    rows, width = own.shape
    return pl.pallas_call(
        functools.partial(aggregate_kernel, parts),
        out_shape=[jax.ShapeDtypeStruct((rows // parts, width), BF16)] * parts,
        in_specs=[VMEM] * 4 + [HBM] * 2 + [SMEM],
        out_specs=[VMEM] * parts,
        scratch_shapes=[
            pltpu.VMEM((3 * rows, width), BF16),
            pltpu.VMEM((rows, width), F32),
            *(pltpu.SMEM(array.shape, jnp.int32) for array in (src, dst)),
            pltpu.SemaphoreType.DMA((2,)),
        ],
        compiler_params=pltpu.CompilerParams(vmem_limit_bytes=GRANT),
        name="aggregate",
    )(own, outer, inner, tiles, src, dst, count)


def convolve(rows_in, w_conv, b_conv, conv, part=slice(None)):
    reached = jnp.dot(rows_in[part], w_conv[...], preferred_element_type=F32) + b_conv[...]
    conv[part] = jnp.maximum(reached, 0.0).astype(BF16)


def bias_of(b_gates, gate, part):
    return b_gates[:, part] + (forget_bias if gate == 1 else 0.0)


def pregate_kernel(rows_in, w_conv, b_conv, w_input, b_gates, *refs):
    pre, _, conv = refs[-3:]
    width = w_input.shape[1] // 4
    convolve(rows_in, w_conv, b_conv, conv)
    for gate in range(4):
        part = slice(gate * width, (gate + 1) * width)
        pre[:, part] = jnp.dot(
            conv[...], w_input[:, part], preferred_element_type=F32
        ) + bias_of(b_gates, gate, part)


def pregate(rows_in, w_conv, b_conv, w_input, b_gates, out):
    rows = rows_in.shape[0]
    depth, gates = w_input.shape
    fresh = isinstance(out, tuple)
    return pl.pallas_call(
        pregate_kernel,
        out_shape=[
            jax.ShapeDtypeStruct((rows, gates), F32),
            jax.ShapeDtypeStruct(out if fresh else out.shape, BF16),
        ],
        in_specs=[VMEM] * 5 + ([] if fresh else [HBM]),
        out_specs=[VMEM, HBM],
        scratch_shapes=[pltpu.VMEM((rows, depth), BF16)],
        input_output_aliases={} if fresh else {5: 1},
        compiler_params=pltpu.CompilerParams(vmem_limit_bytes=GRANT),
        cost_estimate=pl.CostEstimate(
            flops=2 * rows * depth * gates, transcendentals=0, bytes_accessed=rows * gates * 4
        ),
        name="pregate",
    )(rows_in, w_conv, b_conv, w_input, b_gates, *([] if fresh else [out]))


def gate_step(inner, pre, w_input, w_state, b_gates, hidden, cell, target, rows, store_cell=True):
    width = w_state.shape[0]
    chunk = width // 2
    for low in range(0, width, chunk):
        gates = []
        for gate in range(4):
            part = slice(gate * width + low, gate * width + low + chunk)
            if pre is None:
                value = jnp.dot(inner[rows], w_input[:, part], preferred_element_type=F32)
            else:
                value = pre[rows, part]
            if hidden is not None:
                value += jnp.dot(hidden[rows], w_state[:, part], preferred_element_type=F32)
            if pre is None:
                value += bias_of(b_gates, gate, part)
            gates.append(value)
        part = slice(low, low + chunk)
        fresh = (0.5 * jnp.tanh(0.5 * gates[0]) + 0.5) * jnp.tanh(gates[2])
        if hidden is not None:
            fresh += (0.5 * jnp.tanh(0.5 * gates[1]) + 0.5) * cell[rows, part]
        if store_cell:
            cell[rows, part] = fresh
        shown = (0.5 * jnp.tanh(0.5 * gates[3]) + 0.5) * jnp.tanh(fresh)
        target[rows, part] = shown.astype(BF16)


def step_kernel(on_first, on_later, inputs, *refs):
    rows_in, w_conv, b_conv, w_input, w_state, b_gates = refs[:6]
    before = refs[7] if inputs > 7 else None
    _, hidden, cell, conv = refs[inputs:]
    me = lax.axis_index("snap")
    every = slice(None)

    def taken(first):
        convolve(rows_in, w_conv, b_conv, conv)
        source = None if first else before
        gate_step(conv, None, w_input, w_state, b_gates, source, cell, hidden, every)

    for device in on_first:
        pl.when(me == device)(functools.partial(taken, True))
    if on_later is not None:
        pl.when(me >= on_later)(functools.partial(taken, False))


def step(on_first, on_later, rows_in, weights, out, state):
    rows = rows_in.shape[0]
    depth, gates = weights[2].shape
    width = gates // 4
    shape = jax.ShapeDtypeStruct
    operands = [rows_in, *weights, out]
    aliases = {6: 0}
    if state is not None:
        aliases[8] = 2
        if on_later is None:
            aliases[7] = 1
        operands += state
    return pl.pallas_call(
        functools.partial(step_kernel, on_first, on_later, len(operands)),
        out_shape=[shape(out.shape, BF16), shape((rows, width), BF16), shape((rows, width), F32)],
        in_specs=[VMEM] * 6 + [HBM] + [VMEM] * (len(operands) - 7),
        out_specs=[HBM, VMEM, VMEM],
        scratch_shapes=[pltpu.VMEM((rows, depth), BF16)],
        input_output_aliases=aliases,
        compiler_params=pltpu.CompilerParams(vmem_limit_bytes=GRANT),
        cost_estimate=pl.CostEstimate(
            flops=2 * rows * (depth + width) * gates,
            transcendentals=5 * rows * width,
            bytes_accessed=rows * width * 8,
        ),
    )(*operands)


def finish_kernel(snaps, offset, *refs):
    rows_in, w_conv, b_conv, w_input, w_state, b_gates, _, pre = refs[:8]
    out, cell, conv, middle, shown, sems = refs[-6:]
    before = refs[8] if snaps >= 3 else None
    me = lax.axis_index("snap")
    rows = shown.shape[0]
    blocks = LAST_BLOCKS if rows % (16 * LAST_BLOCKS) == 0 else 1
    share = rows // blocks

    def sent(block):
        start = block * share
        return pltpu.make_async_copy(
            shown.at[start : start + share],
            out.at[0, offset + start : offset + start + share],
            sems.at[block],
        )

    def run(source, begins, carried):
        def taken(part):
            convolve(rows_in, w_conv, b_conv, conv, part)
            gate_step(conv, None, w_input, w_state, b_gates, source, cell, middle, part)

        def last(block, part):
            gate_step(None, pre, w_input, w_state, b_gates, carried, cell, shown, part, False)
            sent(block).start()

        parts = [slice(block * share, (block + 1) * share) for block in range(blocks)]
        if begins:
            taken(parts[0])
        for block, part in enumerate(parts):
            if begins and block + 1 < blocks:
                taken(parts[block + 1])
            last(block, part)

    pl.when(me == 0)(functools.partial(run, None, False, None))
    if snaps > 1:
        middle_now = before if snaps == 3 else middle
        pl.when(me == 1)(functools.partial(run, None, snaps != 3, middle_now))
    if snaps > 2:
        pl.when(me > 1)(functools.partial(run, before, True, middle))
    for block in range(blocks):
        sent(block).wait()


def finish(snaps, offset, rows_in, weights, out, pre, state):
    rows = rows_in.shape[0]
    depth, gates = weights[2].shape
    width = gates // 4
    shape = jax.ShapeDtypeStruct
    operands = [rows_in, *weights, out, pre]
    aliases = {6: 0}
    if state is not None:
        aliases[9] = 1
        operands += state
    return pl.pallas_call(
        functools.partial(finish_kernel, snaps, offset),
        out_shape=[shape(out.shape, BF16), shape((rows, width), F32)],
        in_specs=[VMEM] * 6 + [HBM] + [VMEM] * (len(operands) - 7),
        out_specs=[HBM, VMEM],
        scratch_shapes=[
            pltpu.VMEM((rows, depth), BF16),
            pltpu.VMEM((rows, width), BF16),
            pltpu.VMEM((rows, width), BF16),
            pltpu.SemaphoreType.DMA((LAST_BLOCKS,)),
        ],
        input_output_aliases=aliases,
        compiler_params=pltpu.CompilerParams(vmem_limit_bytes=GRANT),
        cost_estimate=pl.CostEstimate(
            flops=2 * rows * (depth + 2 * width) * gates,
            transcendentals=10 * rows * width,
            bytes_accessed=rows * width * 8,
        ),
        name="finish",
    )(*operands)[0]


def shards(
    features,
    adjacency_tiles,
    src_block,
    dst_block,
    block_count,
    w_conv,
    b_conv,
    w_input,
    w_state,
    b_gates,
):
    owners = lax.axis_size("vert")
    snaps = lax.axis_size("snap")
    last = snaps - 1
    odd = [(i, i + 1) for i in range(1, owners - 1, 2)]
    even = [(i, i + 1) for i in range(0, owners - 1, 2)]
    outer = lax.ppermute(features[0], "vert", odd + [(b, a) for a, b in odd])
    inner = lax.ppermute(features[0], "vert", even + [(b, a) for a, b in even])
    own, tiles, *weights = load(
        [features[0], adjacency_tiles[0], w_conv, b_conv[None], w_input, w_state, b_gates[None]]
    )
    w_conv, b_conv, w_input, w_state, b_gates = weights
    lists = [
        pltpu.with_memory_space_constraint(array, pltpu.HBM)
        for array in (src_block, dst_block)
    ]
    halves = aggregate(PARTS, own, outer, inner, tiles, *lists, block_count)
    handed = snaps >= 3

    def shifted(part, hop):
        routes = [(i, i + hop) for i in range(snaps - hop)]
        if handed and hop == last - 1:
            routes = routes[1:]
        return lax.ppermute(halves[part], "snap", routes)

    arrived = {(hop, part): shifted(part, hop) for hop, part in sends(snaps)}
    out = (1, own.shape[0], w_state.shape[0])
    share = own.shape[0] // PARTS
    pre = {}
    for part in range(PARTS):
        pre[part], out = pregate(halves[part], w_conv, b_conv, w_input, b_gates, out)
    passed_back = {}
    states = {part: None for part in range(PARTS)}

    def advance(part, stage):
        hop = snaps - stage
        on_first = [] if stage == 2 else [hop]
        on_later = None if stage == 1 else hop + 1
        out_now, *state = step(on_first, on_later, arrived[hop, part], weights, out, states[part])
        states[part] = state
        return out_now

    def receive_back(part):
        out_now, *state = step([last - 1], None, passed_back[part], weights, out, states[part])
        states[part] = state
        return out_now

    if handed:
        for part in range(PARTS):
            passed_back[part] = lax.ppermute(
                arrived[last, part], "snap", [(last, last - 1)]
            )
            out = advance(part, 1) if snaps > 3 else out
    for part in range(PARTS):
        if snaps == 3:
            out = advance(part, 1)
        for stage in range(2, last):
            out = advance(part, stage)
            if stage == 2:
                out = receive_back(part)
        if snaps == 3:
            out = receive_back(part)
        rows_in = arrived[1, part] if snaps > 1 else halves[part]
        out = finish(
            snaps, part * share, rows_in, weights, out, pre[part], states[part]
        )
    return out


def sends(snaps):
    order = [(snaps - 1, part) for part in range(PARTS)] if snaps > 1 else []
    return order + [(hop, part) for part in range(PARTS) for hop in range(snaps - 2, 0, -1)]


def solution(mesh):
    placed = (
        P("snap", "vert", None),
        P("snap", "vert", None, None),
        P("snap", "vert"),
        P("snap", "vert"),
        P("snap", "vert"),
        P(),
        P(),
        P(),
        P(),
        P(),
    )

    return jax.shard_map(
        shards, mesh=mesh, in_specs=placed, out_specs=P("snap", "vert", None), check_vma=False
    )
```

```python
import functools

import jax
import jax.numpy as jnp
from jax import lax
from jax.experimental import pallas as pl
from jax.experimental.pallas import tpu as pltpu
from jax.sharding import PartitionSpec as P


forget_bias = 2.0
BF16 = jnp.bfloat16
F32 = jnp.float32
VMEM = pl.BlockSpec(memory_space=pltpu.VMEM)
SMEM = pl.BlockSpec(memory_space=pltpu.SMEM)
HBM = pl.BlockSpec(memory_space=pltpu.HBM)
LIST = HBM
GRANT = 24 << 20
PARTS = 1
LAST_BLOCKS = 4


def load_kernel(total, *refs):
    sems = refs[-1]
    copies = []
    for place in range(total):
        copies.append(
            pltpu.make_async_copy(refs[place], refs[total + place], sems.at[place])
        )
    for copy in copies:
        copy.start()
    for copy in copies:
        copy.wait()


def load(arrays):
    bytes_moved = sum(array.size * array.dtype.itemsize for array in arrays)
    return pl.pallas_call(
        functools.partial(load_kernel, len(arrays)),
        out_shape=[jax.ShapeDtypeStruct(array.shape, array.dtype) for array in arrays],
        in_specs=[HBM] * len(arrays),
        out_specs=[VMEM] * len(arrays),
        scratch_shapes=[pltpu.SemaphoreType.DMA((len(arrays),))],
        compiler_params=pltpu.CompilerParams(vmem_limit_bytes=GRANT),
        cost_estimate=pl.CostEstimate(
            flops=0, transcendentals=0, bytes_accessed=2 * bytes_moved
        ),
        name="load",
    )(*(pltpu.with_memory_space_constraint(array, pltpu.HBM) for array in arrays))


def aggregate_kernel(early, own, outer, inner, tiles, src_in, dst_in, count, *refs):
    whole, window, total, src, dst, sems = refs[-6:]
    rows = own.shape[0]
    block = tiles.shape[1]
    slots = tiles.shape[0]
    row_blocks = rows // block
    owner = lax.axis_index("vert")
    base = (owner - 1) * row_blocks
    sender = lax.axis_index("snap") < max(1, lax.axis_size("snap") - 2)

    def run():
        lists = ((src_in, src), (dst_in, dst))
        copies = [pltpu.make_async_copy(a, b, sems.at[i]) for i, (a, b) in enumerate(lists)]
        for copy in copies:
            copy.start()
        window[rows : 2 * rows] = own[...]

        @pl.when(owner % 2 == 0)
        def _():
            window[0:rows] = outer[...]
            window[2 * rows : 3 * rows] = inner[...]

        @pl.when(owner % 2 == 1)
        def _():
            window[0:rows] = inner[...]
            window[2 * rows : 3 * rows] = outer[...]

        total[...] = jnp.zeros_like(total)
        for copy in copies:
            copy.wait()
        products = []
        for slot in range(slots):
            column = jnp.clip(src[0, slot] - base, 0, 3 * row_blocks - 1)
            start = pl.multiple_of(column * block, block)
            products.append(
                jnp.dot(tiles[slot], window[pl.ds(start, block)], preferred_element_type=F32)
            )
        for slot in range(slots):
            start = pl.multiple_of(jnp.clip(dst[0, slot], 0, row_blocks - 1) * block, block)
            alive = slot < count[0, 0]
            total[pl.ds(start, block)] += jnp.where(alive, products[slot], 0.0)
        whole[...] = total[...].astype(BF16)

    if early:
        pl.when(sender)(run)
    else:
        pl.when(jnp.logical_not(sender))(run)

        @pl.when(sender)
        def _():
            whole[...] = refs[0][...]


def aggregate(ready, own, outer, inner, tiles, src, dst, count):
    rows, width = own.shape
    operands = [own, outer, inner, tiles, src, dst, count]
    if ready is not None:
        operands.append(ready)
    return pl.pallas_call(
        functools.partial(aggregate_kernel, ready is None),
        out_shape=jax.ShapeDtypeStruct((rows, width), BF16),
        in_specs=[VMEM] * 4 + [LIST] * 2 + [SMEM] + [VMEM] * (len(operands) - 7),
        out_specs=VMEM,
        scratch_shapes=[
            pltpu.VMEM((3 * rows, width), BF16),
            pltpu.VMEM((rows, width), F32),
            *(pltpu.SMEM(array.shape, jnp.int32) for array in (src, dst)),
            pltpu.SemaphoreType.DMA((2,)),
        ],
        compiler_params=pltpu.CompilerParams(vmem_limit_bytes=GRANT),
        name="aggregate",
    )(*operands)


def convolve(rows_in, w_conv, b_conv, conv, part=slice(None)):
    reached = jnp.dot(rows_in[part], w_conv[...], preferred_element_type=F32) + b_conv[...]
    conv[part] = jnp.maximum(reached, 0.0).astype(BF16)


def bias_of(b_gates, gate, part):
    return b_gates[:, part] + (forget_bias if gate == 1 else 0.0)


def pregate_kernel(rows_in, w_conv, b_conv, w_input, b_gates, *refs):
    pre, _, conv = refs[-3:]
    width = w_input.shape[1] // 4
    convolve(rows_in, w_conv, b_conv, conv)
    for gate in range(4):
        part = slice(gate * width, (gate + 1) * width)
        pre[:, part] = jnp.dot(
            conv[...], w_input[:, part], preferred_element_type=F32
        ) + bias_of(b_gates, gate, part)


def pregate(rows_in, w_conv, b_conv, w_input, b_gates, out):
    rows = rows_in.shape[0]
    depth, gates = w_input.shape
    fresh = isinstance(out, tuple)
    return pl.pallas_call(
        pregate_kernel,
        out_shape=[
            jax.ShapeDtypeStruct((rows, gates), F32),
            jax.ShapeDtypeStruct(out if fresh else out.shape, BF16),
        ],
        in_specs=[VMEM] * 5 + ([] if fresh else [HBM]),
        out_specs=[VMEM, HBM],
        scratch_shapes=[pltpu.VMEM((rows, depth), BF16)],
        input_output_aliases={} if fresh else {5: 1},
        compiler_params=pltpu.CompilerParams(vmem_limit_bytes=GRANT),
        cost_estimate=pl.CostEstimate(
            flops=2 * rows * depth * gates, transcendentals=0, bytes_accessed=rows * gates * 4
        ),
        name="pregate",
    )(rows_in, w_conv, b_conv, w_input, b_gates, *([] if fresh else [out]))


def gate_step(inner, pre, w_input, w_state, b_gates, hidden, cell, target, rows, store_cell=True):
    width = w_state.shape[0]
    chunk = width // 2
    for low in range(0, width, chunk):
        gates = []
        for gate in range(4):
            part = slice(gate * width + low, gate * width + low + chunk)
            if pre is None:
                value = jnp.dot(inner[rows], w_input[:, part], preferred_element_type=F32)
            else:
                value = pre[rows, part]
            if hidden is not None:
                value += jnp.dot(hidden[rows], w_state[:, part], preferred_element_type=F32)
            if pre is None:
                value += bias_of(b_gates, gate, part)
            gates.append(value)
        part = slice(low, low + chunk)
        fresh = (0.5 * jnp.tanh(0.5 * gates[0]) + 0.5) * jnp.tanh(gates[2])
        if hidden is not None:
            fresh += (0.5 * jnp.tanh(0.5 * gates[1]) + 0.5) * cell[rows, part]
        if store_cell:
            cell[rows, part] = fresh
        shown = (0.5 * jnp.tanh(0.5 * gates[3]) + 0.5) * jnp.tanh(fresh)
        target[rows, part] = shown.astype(BF16)


def step_kernel(on_first, on_later, inputs, *refs):
    rows_in, w_conv, b_conv, w_input, w_state, b_gates = refs[:6]
    before = refs[7] if inputs > 7 else None
    _, hidden, cell, conv = refs[inputs:]
    me = lax.axis_index("snap")
    every = slice(None)

    def taken(first):
        convolve(rows_in, w_conv, b_conv, conv)
        source = None if first else before
        gate_step(conv, None, w_input, w_state, b_gates, source, cell, hidden, every)

    for device in on_first:
        pl.when(me == device)(functools.partial(taken, True))
    if on_later is not None:
        pl.when(me >= on_later)(functools.partial(taken, False))


def step(on_first, on_later, rows_in, weights, out, state):
    rows = rows_in.shape[0]
    depth, gates = weights[2].shape
    width = gates // 4
    shape = jax.ShapeDtypeStruct
    operands = [rows_in, *weights, out]
    aliases = {6: 0}
    if state is not None:
        aliases[8] = 2
        if on_later is None:
            aliases[7] = 1
        operands += state
    return pl.pallas_call(
        functools.partial(step_kernel, on_first, on_later, len(operands)),
        out_shape=[shape(out.shape, BF16), shape((rows, width), BF16), shape((rows, width), F32)],
        in_specs=[VMEM] * 6 + [HBM] + [VMEM] * (len(operands) - 7),
        out_specs=[HBM, VMEM, VMEM],
        scratch_shapes=[pltpu.VMEM((rows, depth), BF16)],
        input_output_aliases=aliases,
        compiler_params=pltpu.CompilerParams(vmem_limit_bytes=GRANT),
        cost_estimate=pl.CostEstimate(
            flops=2 * rows * (depth + width) * gates,
            transcendentals=5 * rows * width,
            bytes_accessed=rows * width * 8,
        ),
    )(*operands)


def finish_kernel(snaps, offset, *refs):
    rows_in, w_conv, b_conv, w_input, w_state, b_gates, _, pre = refs[:8]
    out, cell, conv, middle, shown, sems = refs[-6:]
    before = refs[8] if snaps >= 3 else None
    me = lax.axis_index("snap")
    rows = shown.shape[0]
    blocks = LAST_BLOCKS if rows % (16 * LAST_BLOCKS) == 0 else 1
    share = rows // blocks

    def sent(block):
        start = block * share
        return pltpu.make_async_copy(
            shown.at[start : start + share],
            out.at[0, offset + start : offset + start + share],
            sems.at[block],
        )

    def run(source, begins, carried):
        def taken(part):
            convolve(rows_in, w_conv, b_conv, conv, part)
            gate_step(conv, None, w_input, w_state, b_gates, source, cell, middle, part)

        def last(block, part):
            gate_step(None, pre, w_input, w_state, b_gates, carried, cell, shown, part, False)
            sent(block).start()

        parts = [slice(block * share, (block + 1) * share) for block in range(blocks)]
        if begins:
            taken(parts[0])
        for block, part in enumerate(parts):
            if begins and block + 1 < blocks:
                taken(parts[block + 1])
            last(block, part)

    pl.when(me == 0)(functools.partial(run, None, False, None))
    if snaps > 1:
        middle_now = before if snaps == 3 else middle
        pl.when(me == 1)(functools.partial(run, None, snaps != 3, middle_now))
    if snaps > 2:
        pl.when(me > 1)(functools.partial(run, before, True, middle))
    for block in range(blocks):
        sent(block).wait()


def finish(snaps, offset, rows_in, weights, out, pre, state):
    rows = rows_in.shape[0]
    depth, gates = weights[2].shape
    width = gates // 4
    shape = jax.ShapeDtypeStruct
    operands = [rows_in, *weights, out, pre]
    aliases = {6: 0}
    if state is not None:
        aliases[9] = 1
        operands += state
    return pl.pallas_call(
        functools.partial(finish_kernel, snaps, offset),
        out_shape=[shape(out.shape, BF16), shape((rows, width), F32)],
        in_specs=[VMEM] * 6 + [HBM] + [VMEM] * (len(operands) - 7),
        out_specs=[HBM, VMEM],
        scratch_shapes=[
            pltpu.VMEM((rows, depth), BF16),
            pltpu.VMEM((rows, width), BF16),
            pltpu.VMEM((rows, width), BF16),
            pltpu.SemaphoreType.DMA((LAST_BLOCKS,)),
        ],
        input_output_aliases=aliases,
        compiler_params=pltpu.CompilerParams(vmem_limit_bytes=GRANT),
        cost_estimate=pl.CostEstimate(
            flops=2 * rows * (depth + 2 * width) * gates,
            transcendentals=10 * rows * width,
            bytes_accessed=rows * width * 8,
        ),
        name="finish",
    )(*operands)[0]


def shards(
    features,
    adjacency_tiles,
    src_block,
    dst_block,
    block_count,
    w_conv,
    b_conv,
    w_input,
    w_state,
    b_gates,
):
    owners = lax.axis_size("vert")
    snaps = lax.axis_size("snap")
    last = snaps - 1
    odd = [(i, i + 1) for i in range(1, owners - 1, 2)]
    even = [(i, i + 1) for i in range(0, owners - 1, 2)]
    outer = lax.ppermute(features[0], "vert", odd + [(b, a) for a, b in odd])
    inner = lax.ppermute(features[0], "vert", even + [(b, a) for a, b in even])
    own, tiles, *weights = load(
        [features[0], adjacency_tiles[0], w_conv, b_conv[None], w_input, w_state, b_gates[None]]
    )
    w_conv, b_conv, w_input, w_state, b_gates = weights
    lists = [
        pltpu.with_memory_space_constraint(array, pltpu.HBM)
        for array in (src_block, dst_block)
    ]
    ready = aggregate(None, own, outer, inner, tiles, *lists, block_count)
    handed = snaps >= 3

    def shifted(hop):
        routes = [(i, i + hop) for i in range(snaps - hop)]
        if handed and hop == last - 1:
            routes = routes[1:]
        return lax.ppermute(ready if hop > 1 else whole, "snap", routes)

    arrived = {}
    for hop, part in sends(snaps):
        if hop > 1:
            arrived[hop, part] = shifted(hop)
    whole = aggregate(ready, own, outer, inner, tiles, *lists, block_count)
    halves = [whole]
    for hop, part in sends(snaps):
        if (hop, part) not in arrived:
            arrived[hop, part] = shifted(hop)
    out = (1, own.shape[0], w_state.shape[0])
    share = own.shape[0] // PARTS
    pre = {}
    for part in range(PARTS):
        pre[part], out = pregate(halves[part], w_conv, b_conv, w_input, b_gates, out)
    passed_back = {}
    states = {part: None for part in range(PARTS)}

    def advance(part, stage):
        hop = snaps - stage
        on_first = [] if stage == 2 else [hop]
        on_later = None if stage == 1 else hop + 1
        out_now, *state = step(on_first, on_later, arrived[hop, part], weights, out, states[part])
        states[part] = state
        return out_now

    def receive_back(part):
        out_now, *state = step([last - 1], None, passed_back[part], weights, out, states[part])
        states[part] = state
        return out_now

    if handed:
        for part in range(PARTS):
            passed_back[part] = lax.ppermute(
                arrived[last, part], "snap", [(last, last - 1)]
            )
            out = advance(part, 1) if snaps > 3 else out
    for part in range(PARTS):
        if snaps == 3:
            out = advance(part, 1)
        for stage in range(2, last):
            out = advance(part, stage)
            if stage == 2:
                out = receive_back(part)
        if snaps == 3:
            out = receive_back(part)
        rows_in = arrived[1, part] if snaps > 1 else halves[part]
        out = finish(
            snaps, part * share, rows_in, weights, out, pre[part], states[part]
        )
    return out


def sends(snaps):
    order = [(snaps - 1, part) for part in range(PARTS)] if snaps > 1 else []
    return order + [(hop, part) for part in range(PARTS) for hop in range(snaps - 2, 0, -1)]


def solution(mesh):
    placed = (
        P("snap", "vert", None),
        P("snap", "vert", None, None),
        P("snap", "vert"),
        P("snap", "vert"),
        P("snap", "vert"),
        P(),
        P(),
        P(),
        P(),
        P(),
    )

    return jax.shard_map(
        shards, mesh=mesh, in_specs=placed, out_specs=P("snap", "vert", None), check_vma=False
    )
```

```python
import functools

import jax
import jax.numpy as jnp
from jax import lax
from jax.experimental import pallas as pl
from jax.experimental.pallas import tpu as pltpu
from jax.sharding import PartitionSpec as P


forget_bias = 2.0
BF16 = jnp.bfloat16
F32 = jnp.float32
VMEM = pl.BlockSpec(memory_space=pltpu.VMEM)
SMEM = pl.BlockSpec(memory_space=pltpu.SMEM)
HBM = pl.BlockSpec(memory_space=pltpu.HBM)
LIST = HBM
GRANT = 24 << 20
PARTS = 1
LAST_BLOCKS = 4


def load_kernel(total, *refs):
    sems = refs[-1]
    copies = []
    for place in range(total):
        copies.append(
            pltpu.make_async_copy(refs[place], refs[total + place], sems.at[place])
        )
    for copy in copies:
        copy.start()
    for copy in copies:
        copy.wait()


def load(arrays):
    bytes_moved = sum(array.size * array.dtype.itemsize for array in arrays)
    return pl.pallas_call(
        functools.partial(load_kernel, len(arrays)),
        out_shape=[jax.ShapeDtypeStruct(array.shape, array.dtype) for array in arrays],
        in_specs=[HBM] * len(arrays),
        out_specs=[VMEM] * len(arrays),
        scratch_shapes=[pltpu.SemaphoreType.DMA((len(arrays),))],
        compiler_params=pltpu.CompilerParams(vmem_limit_bytes=GRANT),
        cost_estimate=pl.CostEstimate(
            flops=0, transcendentals=0, bytes_accessed=2 * bytes_moved
        ),
        name="load",
    )(*(pltpu.with_memory_space_constraint(array, pltpu.HBM) for array in arrays))


def aggregate_kernel(early, own, outer, inner, tiles, src_in, dst_in, count, *refs):
    whole, window, total, src, dst, sems = refs[-6:]
    rows = own.shape[0]
    block = tiles.shape[1]
    slots = tiles.shape[0]
    row_blocks = rows // block
    owner = lax.axis_index("vert")
    base = (owner - 1) * row_blocks
    sender = lax.axis_index("snap") < max(1, lax.axis_size("snap") - 2)

    def run():
        lists = ((src_in, src), (dst_in, dst))
        copies = [pltpu.make_async_copy(a, b, sems.at[i]) for i, (a, b) in enumerate(lists)]
        for copy in copies:
            copy.start()
        window[rows : 2 * rows] = own[...]

        @pl.when(owner % 2 == 0)
        def _():
            window[0:rows] = outer[...]
            window[2 * rows : 3 * rows] = inner[...]

        @pl.when(owner % 2 == 1)
        def _():
            window[0:rows] = inner[...]
            window[2 * rows : 3 * rows] = outer[...]

        total[...] = jnp.zeros_like(total)
        for copy in copies:
            copy.wait()
        products = []
        for slot in range(slots):
            column = jnp.clip(src[0, slot] - base, 0, 3 * row_blocks - 1)
            start = pl.multiple_of(column * block, block)
            products.append(
                jnp.dot(tiles[slot], window[pl.ds(start, block)], preferred_element_type=F32)
            )
        for slot in range(slots):
            start = pl.multiple_of(jnp.clip(dst[0, slot], 0, row_blocks - 1) * block, block)
            alive = slot < count[0, 0]
            total[pl.ds(start, block)] += jnp.where(alive, products[slot], 0.0)
        whole[...] = total[...].astype(BF16)

    if early:
        pl.when(sender)(run)
    else:
        pl.when(jnp.logical_not(sender))(run)

        @pl.when(sender)
        def _():
            whole[...] = refs[0][...]


def aggregate(ready, own, outer, inner, tiles, src, dst, count):
    rows, width = own.shape
    operands = [own, outer, inner, tiles, src, dst, count]
    if ready is not None:
        operands.append(ready)
    return pl.pallas_call(
        functools.partial(aggregate_kernel, ready is None),
        out_shape=jax.ShapeDtypeStruct((rows, width), BF16),
        in_specs=[VMEM] * 4 + [LIST] * 2 + [SMEM] + [VMEM] * (len(operands) - 7),
        out_specs=VMEM,
        scratch_shapes=[
            pltpu.VMEM((3 * rows, width), BF16),
            pltpu.VMEM((rows, width), F32),
            *(pltpu.SMEM(array.shape, jnp.int32) for array in (src, dst)),
            pltpu.SemaphoreType.DMA((2,)),
        ],
        compiler_params=pltpu.CompilerParams(vmem_limit_bytes=GRANT),
        name="aggregate",
    )(*operands)


def convolve(rows_in, w_conv, b_conv, conv, part=slice(None)):
    reached = jnp.dot(rows_in[part], w_conv[...], preferred_element_type=F32) + b_conv[...]
    conv[part] = jnp.maximum(reached, 0.0).astype(BF16)


def bias_of(b_gates, gate, part):
    return b_gates[:, part] + (forget_bias if gate == 1 else 0.0)


def pregate_kernel(rows_in, w_conv, b_conv, w_input, b_gates, *refs):
    pre, _, conv = refs[-3:]
    width = w_input.shape[1] // 4
    convolve(rows_in, w_conv, b_conv, conv)
    for gate in range(4):
        part = slice(gate * width, (gate + 1) * width)
        pre[:, part] = jnp.dot(
            conv[...], w_input[:, part], preferred_element_type=F32
        ) + bias_of(b_gates, gate, part)


def pregate(rows_in, w_conv, b_conv, w_input, b_gates, out):
    rows = rows_in.shape[0]
    depth, gates = w_input.shape
    fresh = isinstance(out, tuple)
    return pl.pallas_call(
        pregate_kernel,
        out_shape=[
            jax.ShapeDtypeStruct((rows, gates), F32),
            jax.ShapeDtypeStruct(out if fresh else out.shape, BF16),
        ],
        in_specs=[VMEM] * 5 + ([] if fresh else [HBM]),
        out_specs=[VMEM, HBM],
        scratch_shapes=[pltpu.VMEM((rows, depth), BF16)],
        input_output_aliases={} if fresh else {5: 1},
        compiler_params=pltpu.CompilerParams(vmem_limit_bytes=GRANT),
        cost_estimate=pl.CostEstimate(
            flops=2 * rows * depth * gates, transcendentals=0, bytes_accessed=rows * gates * 4
        ),
        name="pregate",
    )(rows_in, w_conv, b_conv, w_input, b_gates, *([] if fresh else [out]))


def gate_step(inner, pre, w_input, w_state, b_gates, hidden, held, cell, target, rows):
    width = w_state.shape[0]
    chunk = width // 2
    for low in range(0, width, chunk):
        gates = []
        for gate in range(4):
            part = slice(gate * width + low, gate * width + low + chunk)
            if pre is None:
                value = jnp.dot(inner[rows], w_input[:, part], preferred_element_type=F32)
            else:
                value = pre[rows, part]
            if hidden is not None:
                value += jnp.dot(hidden[rows], w_state[:, part], preferred_element_type=F32)
            if pre is None:
                value += bias_of(b_gates, gate, part)
            gates.append(value)
        part = slice(low, low + chunk)
        fresh = (0.5 * jnp.tanh(0.5 * gates[0]) + 0.5) * jnp.tanh(gates[2])
        if hidden is not None:
            fresh += (0.5 * jnp.tanh(0.5 * gates[1]) + 0.5) * held[rows, part]
        if cell is not None:
            cell[rows, part] = fresh
        shown = (0.5 * jnp.tanh(0.5 * gates[3]) + 0.5) * jnp.tanh(fresh)
        target[rows, part] = shown.astype(BF16)


def step_kernel(on_first, on_later, inputs, *refs):
    rows_in, w_conv, b_conv, w_input, w_state, b_gates = refs[:6]
    before, held = refs[7:9] if inputs > 7 else (None, None)
    _, hidden, cell, conv = refs[inputs:]
    me = lax.axis_index("snap")
    every = slice(None)

    def taken(first):
        convolve(rows_in, w_conv, b_conv, conv)
        source = None if first else before
        gate_step(conv, None, w_input, w_state, b_gates, source, held, cell, hidden, every)

    for device in on_first:
        pl.when(me == device)(functools.partial(taken, True))
    if on_later is not None:
        pl.when(me >= on_later)(functools.partial(taken, False))
    elif before is not None:

        @pl.when(me > on_first[0])
        def _():
            hidden[...] = before[...]
            cell[...] = held[...]


def step(on_first, on_later, rows_in, weights, out, state):
    rows = rows_in.shape[0]
    depth, gates = weights[2].shape
    width = gates // 4
    shape = jax.ShapeDtypeStruct
    operands = [rows_in, *weights, out]
    aliases = {6: 0}
    if state is not None:
        aliases[8] = 2
        if on_later is None:
            aliases[7] = 1
        operands += state
    return pl.pallas_call(
        functools.partial(step_kernel, on_first, on_later, len(operands)),
        out_shape=[shape(out.shape, BF16), shape((rows, width), BF16), shape((rows, width), F32)],
        in_specs=[VMEM] * 6 + [HBM] + [VMEM] * (len(operands) - 7),
        out_specs=[HBM, VMEM, VMEM],
        scratch_shapes=[pltpu.VMEM((rows, depth), BF16)],
        input_output_aliases=aliases,
        compiler_params=pltpu.CompilerParams(vmem_limit_bytes=GRANT),
        cost_estimate=pl.CostEstimate(
            flops=2 * rows * (depth + width) * gates,
            transcendentals=5 * rows * width,
            bytes_accessed=rows * width * 8,
        ),
    )(*operands)


def finish_kernel(snaps, offset, *refs):
    rows_in, w_conv, b_conv, w_input, w_state, b_gates, _, pre = refs[:8]
    out, cell, conv, middle, shown, sems = refs[-6:]
    before, held = refs[8:10] if snaps >= 3 else (None, None)
    me = lax.axis_index("snap")
    rows = shown.shape[0]
    blocks = LAST_BLOCKS if rows % (16 * LAST_BLOCKS) == 0 else 1
    share = rows // blocks

    def sent(block):
        start = block * share
        return pltpu.make_async_copy(
            shown.at[start : start + share],
            out.at[0, offset + start : offset + start + share],
            sems.at[block],
        )

    def run(source, begins, carried, kept):
        def taken(part):
            convolve(rows_in, w_conv, b_conv, conv, part)
            gate_step(conv, None, w_input, w_state, b_gates, source, held, cell, middle, part)

        def last(block, part):
            gate_step(None, pre, w_input, w_state, b_gates, carried, kept, None, shown, part)
            sent(block).start()

        parts = [slice(block * share, (block + 1) * share) for block in range(blocks)]
        if begins:
            taken(parts[0])
        for block, part in enumerate(parts):
            if begins and block + 1 < blocks:
                taken(parts[block + 1])
            last(block, part)

    pl.when(me == 0)(functools.partial(run, None, False, None, None))
    if snaps > 1:
        carried, kept = (before, held) if snaps == 3 else (middle, cell)
        pl.when(me == 1)(functools.partial(run, None, snaps != 3, carried, kept))
    if snaps > 2:
        pl.when(me > 1)(functools.partial(run, before, True, middle, cell))
    for block in range(blocks):
        sent(block).wait()


def finish(snaps, offset, rows_in, weights, out, pre, state):
    rows = rows_in.shape[0]
    depth, gates = weights[2].shape
    width = gates // 4
    shape = jax.ShapeDtypeStruct
    operands = [rows_in, *weights, out, pre]
    aliases = {6: 0}
    if state is not None:
        aliases[9] = 1
        operands += state
    return pl.pallas_call(
        functools.partial(finish_kernel, snaps, offset),
        out_shape=[shape(out.shape, BF16), shape((rows, width), F32)],
        in_specs=[VMEM] * 6 + [HBM] + [VMEM] * (len(operands) - 7),
        out_specs=[HBM, VMEM],
        scratch_shapes=[
            pltpu.VMEM((rows, depth), BF16),
            pltpu.VMEM((rows, width), BF16),
            pltpu.VMEM((rows, width), BF16),
            pltpu.SemaphoreType.DMA((LAST_BLOCKS,)),
        ],
        input_output_aliases=aliases,
        compiler_params=pltpu.CompilerParams(vmem_limit_bytes=GRANT),
        cost_estimate=pl.CostEstimate(
            flops=2 * rows * (depth + 2 * width) * gates,
            transcendentals=10 * rows * width,
            bytes_accessed=rows * width * 8,
        ),
        name="finish",
    )(*operands)[0]


def shards(
    features,
    adjacency_tiles,
    src_block,
    dst_block,
    block_count,
    w_conv,
    b_conv,
    w_input,
    w_state,
    b_gates,
):
    owners = lax.axis_size("vert")
    snaps = lax.axis_size("snap")
    last = snaps - 1
    odd = [(i, i + 1) for i in range(1, owners - 1, 2)]
    even = [(i, i + 1) for i in range(0, owners - 1, 2)]
    outer = lax.ppermute(features[0], "vert", odd + [(b, a) for a, b in odd])
    inner = lax.ppermute(features[0], "vert", even + [(b, a) for a, b in even])
    own, tiles, *weights = load(
        [features[0], adjacency_tiles[0], w_conv, b_conv[None], w_input, w_state, b_gates[None]]
    )
    w_conv, b_conv, w_input, w_state, b_gates = weights
    lists = [
        pltpu.with_memory_space_constraint(array, pltpu.HBM)
        for array in (src_block, dst_block)
    ]
    ready = aggregate(None, own, outer, inner, tiles, *lists, block_count)
    handed = snaps >= 3

    def shifted(hop):
        routes = [(i, i + hop) for i in range(snaps - hop)]
        if handed and hop == last - 1:
            routes = routes[1:]
        return lax.ppermute(ready if hop > 1 else whole, "snap", routes)

    arrived = {}
    for hop, part in sends(snaps):
        if hop > 1:
            arrived[hop, part] = shifted(hop)
    whole = aggregate(ready, own, outer, inner, tiles, *lists, block_count)
    halves = [whole]
    for hop, part in sends(snaps):
        if (hop, part) not in arrived:
            arrived[hop, part] = shifted(hop)
    out = (1, own.shape[0], w_state.shape[0])
    share = own.shape[0] // PARTS
    pre = {}
    for part in range(PARTS):
        pre[part], out = pregate(halves[part], w_conv, b_conv, w_input, b_gates, out)
    passed_back = {}
    states = {part: None for part in range(PARTS)}

    def advance(part, stage):
        hop = snaps - stage
        on_first = [] if stage == 2 else [hop]
        on_later = None if stage == 1 else hop + 1
        out_now, *state = step(on_first, on_later, arrived[hop, part], weights, out, states[part])
        states[part] = state
        return out_now

    def receive_back(part):
        out_now, *state = step([last - 1], None, passed_back[part], weights, out, states[part])
        states[part] = state
        return out_now

    if handed:
        for part in range(PARTS):
            passed_back[part] = lax.ppermute(
                arrived[last, part], "snap", [(last, last - 1)]
            )
            out = advance(part, 1) if snaps > 3 else out
    for part in range(PARTS):
        if snaps == 3:
            out = advance(part, 1)
        for stage in range(2, last):
            out = advance(part, stage)
            if stage == 2:
                out = receive_back(part)
        if snaps == 3:
            out = receive_back(part)
        rows_in = arrived[1, part] if snaps > 1 else halves[part]
        out = finish(
            snaps, part * share, rows_in, weights, out, pre[part], states[part]
        )
    return out


def sends(snaps):
    order = [(snaps - 1, part) for part in range(PARTS)] if snaps > 1 else []
    return order + [(hop, part) for part in range(PARTS) for hop in range(snaps - 2, 0, -1)]


def solution(mesh):
    placed = (
        P("snap", "vert", None),
        P("snap", "vert", None, None),
        P("snap", "vert"),
        P("snap", "vert"),
        P("snap", "vert"),
        P(),
        P(),
        P(),
        P(),
        P(),
    )

    return jax.shard_map(
        shards, mesh=mesh, in_specs=placed, out_specs=P("snap", "vert", None), check_vma=False
    )
```
